32 devices in a mesh: groups: 2 (over x), lon: 16 (over z, y, core).
Axes of the slice: x: 2, y: 2, z: 4, core: 2. Of those that a mesh axis runs over, the one named last changes fastest.
Arguments:
- tracers: bfloat16 [2048, 64, 256], P(('groups', 'lon')), parts along dimension 0, may hold values from -6 to 6
- wind_fields: bfloat16 [2048, 64, 128], P(('groups', 'lon')), parts along dimension 0, may hold values from -3 to 3
- departures: int32 [32, 16, 2], P(('groups', 'lon')), parts along dimension 0, may hold values from -4 to 3, as said below
Outputs:
- advected: bfloat16 [2048, 64, 256], P(('groups', 'lon')), parts along dimension 0
The draws below stay inside these ranges and needn't reach their ends.
There are 2 independent parts, one for each index of `groups`. The reference program is written for one: setup_inputs(seed, part) draws one part's arguments, and reference() takes and returns one part's arrays. A program takes and returns all parts, laid end to end along the dimension named above; each array names one. Nothing has to cross between parts.
Inputs may be any that keep to these rules, and one draw needn't show every extreme that they name: `departures`: entry 0 lies in -4..3 and entry 1 in -1..1 with q - entry 1 a valid band; in every sector exactly 4 bands share one value of entry 0, and no value is shared by more.
All inputs are finite; a program needn't handle non-finite values.
Results may differ from the reference program's by a relative error of at most 0.001.
Values may be sent and summed in bfloat16 or wider, within the bound.
A program may use at most 128 MiB of HBM per device.

```python
import jax
import jax.numpy as jnp
from jax import lax

NTRACER = 8
LEVELS = 32
CLON = 64
BR = 4
NB = 16
CAP = 4
TRAJ = 3
NLON = 1024
NLAT = 64
TCH = 256
N_LON = 16


def draw_departures(key, part):
    base_key = jax.random.fold_in(key, 7)
    sector_key, lat_key = jax.random.split(base_key, 2)

    def sector_draw(key_sector):
        first_key, second_key, third_key = jax.random.split(key_sector, 3)
        ordering = jax.random.permutation(first_key, jnp.arange(8, dtype=jnp.int32))
        remaining = jnp.repeat(ordering[1:], CAP - 1)
        remaining = jax.random.permutation(second_key, remaining)
        chosen = jnp.concatenate([jnp.full((CAP,), ordering[0], jnp.int32), remaining[:NB - CAP]])
        chosen = jax.random.permutation(third_key, chosen)
        return chosen - 4
    lon_tiles = jax.vmap(sector_draw)(jax.random.split(sector_key, N_LON))
    band_ids = jnp.arange(NB, dtype=jnp.int32)[None, :]
    lat_tiles = jax.random.randint(lat_key, (N_LON, NB), -1, 2, dtype=jnp.int32)
    lat_tiles = jnp.clip(lat_tiles, band_ids - NB + 1, band_ids)
    return jnp.stack([lon_tiles, lat_tiles], -1).astype(jnp.int32)


def level_of(own_key, shape, pieces, least, top_value):
    def one(axis_at, shards_of):
        heights = jax.random.uniform(jax.random.fold_in(jax.random.fold_in(own_key, 6), axis_at), (shards_of,), jnp.float32, least / len(pieces), top_value / len(pieces))
        return jnp.repeat(jnp.exp(heights), shape[axis_at] // shards_of).reshape((-1,) + (1,) * (len(shape) - axis_at - 1))

    factor_of = one(*pieces[0])
    for cut in pieces[1:]:
        factor_of = factor_of * one(*cut)
    return factor_of


def scatter_about(rng, extent, deviation, limit, cuts=(), kind=jnp.bfloat16):
    values = jax.random.normal(rng, extent, jnp.float32) * deviation
    if len(cuts) > 0:
        values = level_of(rng, extent, cuts, -0.22, 0.18) * values
    return jnp.clip(values, min=-limit, max=limit).astype(kind)


def setup_inputs(seed: int = 0, part: int = 0) -> dict:
    streams_of = jax.random.split(jax.random.key(seed), 4)
    part_keys = jax.random.split(jax.random.fold_in(streams_of[3], part), 4)
    tracers = scatter_about(part_keys[0], (NLON, NLAT, TCH), 1.0, 6.0, ((0, 16),))
    wind_fields = scatter_about(part_keys[1], (NLON, NLAT, 4 * LEVELS), 0.5, 3.0, ((0, 16),))
    departures = draw_departures(jax.random.fold_in(jax.random.fold_in(streams_of[3], part), 71), part)
    return {"tracers": tracers, "wind_fields": wind_fields, "departures": departures}


CLIP_BOUND = 0.95


def linear_kernel(distance):
    return jnp.maximum(1.0 - jnp.abs(distance), 0.0)


def cubic_kernel(distance):
    magnitude = jnp.abs(distance)
    inner_part = 0.5 * (1.0 - magnitude) * (2.0 - magnitude) * (1.0 + magnitude)
    outer_part = -(magnitude - 1.0) * (2.0 - magnitude) * (3.0 - magnitude) / 6.0
    return jnp.where(magnitude < 1.0, inner_part, jnp.where(magnitude < 2.0, outer_part, 0.0))


def advect_tile(source_tile, arrival_wind):
    columns = source_tile.shape[0] - 4
    band_rows = source_tile.shape[1] - 4
    levels = arrival_wind.shape[-1] // 2
    tracer_ch = source_tile.shape[-1] - 4 * levels
    per_level = tracer_ch // levels
    wind_data = source_tile[:, :, tracer_ch:].astype(jnp.float32)
    extrapolated = 2.0 * wind_data[:, :, :2 * levels] - wind_data[:, :, 2 * levels:]
    wind_here = arrival_wind.astype(jnp.float32)
    displace = jnp.clip(wind_here, -CLIP_BOUND, CLIP_BOUND)
    for iteration in range(TRAJ):
        lon_shift = displace[:, :, :levels]
        lat_shift = displace[:, :, levels:]
        accumulated = jnp.zeros_like(wind_here)
        for lat_step in (-1, 0, 1):
            lat_weight = linear_kernel(lat_step + lat_shift)
            for lon_step in (-1, 0, 1):
                weight = linear_kernel(lon_step + lon_shift) * lat_weight
                window = extrapolated[2 + lon_step:2 + lon_step + columns, 2 + lat_step:2 + lat_step + band_rows, :]
                accumulated = accumulated + jnp.concatenate([weight, weight], -1) * window
        displace = jnp.clip(0.5 * (wind_here + accumulated), -CLIP_BOUND, CLIP_BOUND)
    lon_shift = displace[:, :, :levels]
    lat_shift = displace[:, :, levels:]
    result = jnp.zeros((columns, band_rows, tracer_ch), jnp.float32)
    for lat_step in range(-2, 3):
        lat_dist = lat_step + lat_shift
        lat_weight = cubic_kernel(lat_dist)
        inner_rows = jnp.abs(lat_dist) < 1.0
        for lon_step in range(-2, 3):
            lon_dist = lon_step + lon_shift
            lon_weight = jnp.where(inner_rows, cubic_kernel(lon_dist), linear_kernel(lon_dist))
            weight = jnp.repeat(lon_weight * lat_weight, per_level, axis=-1)
            window = source_tile[2 + lon_step:2 + lon_step + columns, 2 + lat_step:2 + lat_step + band_rows, :tracer_ch]
            result = result + weight * window.astype(jnp.float32)
    return result.astype(jnp.bfloat16)


def reference(tracers, wind_fields, departures):
    combined = jnp.concatenate([tracers, wind_fields], -1)
    padded = jnp.concatenate([combined[:, :1], combined[:, :1], combined, combined[:, -1:], combined[:, -1:]], 1)
    padded = jnp.concatenate([padded[-2:], padded, padded[:2]], 0)
    channels = combined.shape[-1]

    def advect_one(tile_index):
        sector = tile_index // NB
        band_index = tile_index % NB
        lon_tiles = departures[sector, band_index, 0]
        lat_tiles = departures[sector, band_index, 1]
        source = ((sector - lon_tiles) % N_LON).astype(jnp.int32)
        source_band = (band_index - lat_tiles).astype(jnp.int32)
        zero_index = jnp.zeros((), jnp.int32)
        source_tile = lax.dynamic_slice(padded, (source * CLON, source_band * BR, zero_index), (CLON + 4, BR + 4, channels))
        arrival_wind = lax.dynamic_slice(wind_fields, (sector * CLON, band_index * BR, zero_index), (CLON, BR, 2 * LEVELS))
        return advect_tile(source_tile, arrival_wind)

    moved = lax.map(advect_one, jnp.arange(N_LON * NB, dtype=jnp.int32))
    moved = moved.reshape(N_LON, NB, CLON, BR, LEVELS * NTRACER)
    moved = jnp.transpose(moved, (0, 2, 1, 3, 4))
    return moved.reshape(N_LON * CLON, NB * BR, LEVELS * NTRACER)
```

```python
import functools

import jax
import jax.numpy as jnp
from jax import lax
from jax.experimental import pallas as pl
from jax.experimental.pallas import tpu as pltpu
from jax.sharding import PartitionSpec as P

CAP = 4
TRAJ = 3
CLIP_BOUND = 0.95
LOW, HIGH = -3, 4
CHUNKS = 8
MESH = pl.DeviceIdType.MESH


def linear_kernel(distance):
    return jnp.maximum(1.0 - jnp.abs(distance), 0.0)


def linear_near(r):
    return [jnp.maximum(r, 0.0), 1.0 - jnp.abs(r), jnp.maximum(-r, 0.0)]


def cubic_all(r):
    t = jnp.abs(r)
    u = 1.0 - t
    v = 1.0 + t
    w = 2.0 - t
    uw = u * w
    tv = t * v
    near0 = 0.5 * (uw * v)
    near1 = 0.5 * (tv * w)
    far1 = (-1.0 / 6.0) * (uw * t)
    far2 = (-1.0 / 6.0) * (tv * u)
    pos = r > 0.0
    zero = jnp.zeros_like(t)
    return [
        jnp.where(pos, far2, zero),
        jnp.where(pos, near1, far1),
        near0,
        jnp.where(pos, far1, near1),
        jnp.where(pos, zero, far2),
    ]


def place(dep_ref, band, rows, total_rows):
    source = band - dep_ref[band, 1]
    first = source * rows - 2
    base = jnp.clip((first + 8) // 8 * 8 - 8, 0, total_rows - 16)
    return base, first - base


def advect_kernel(columns, rows, levels, dep_ref, here_ref, wt_ref, ww_ref, out_ref,
                  tbuf, wbuf, t8, w8, s_ref, p_ref, r_ref, d_ref, e_ref, sems):
    g = pl.program_id(0)
    steps = pl.num_programs(0)
    total_rows = wt_ref.shape[1]
    width = columns + 4
    tracer_ch = wt_ref.shape[2]
    lane_tiles = tracer_ch // 128
    half = columns // 2
    slot = lax.rem(g, 2)

    def copies(step, where, j):
        band = step * 2 + j
        base, _ = place(dep_ref, band, rows, total_rows)
        start = (HIGH - 1 - dep_ref[band, 0]) * columns
        at = (pl.ds(start, width), pl.ds(pl.multiple_of(base, 8), 16), slice(None))
        return (
            pltpu.make_async_copy(wt_ref.at[at], tbuf.at[where, j], sems.at[where, j, 0]),
            pltpu.make_async_copy(ww_ref.at[at], wbuf.at[where, j], sems.at[where, j, 1]),
        )

    @pl.when(g == 0)
    def _():
        for j in range(2):
            for c in copies(0, 0, j):
                c.start()
        row = lax.broadcasted_iota(jnp.int32, e_ref.shape, 0)
        col = lax.broadcasted_iota(jnp.int32, e_ref.shape, 1)
        part = col // tracer_ch
        level = (col % tracer_ch) // (tracer_ch // levels)
        hit = (row % 128) == part * levels + level
        e_ref[...] = jnp.where(hit, 1.0, 0.0).astype(e_ref.dtype)

    @pl.when(g + 1 < steps)
    def _():
        for j in range(2):
            for c in copies(g + 1, 1 - slot, j):
                c.start()

    for j in range(2):
        for c in copies(g, slot, j):
            c.wait()

    def cut(x, off):
        if off < 0:
            return jnp.concatenate([x[:, :1]] * (-off) + [x[:, : 8 + off]], axis=1)
        if off + 8 > 16:
            return jnp.concatenate([x[:, off:]] + [x[:, 15:]] * (off - 8), axis=1)
        return x[:, off : off + 8]

    for j in range(2):
        _, offset = place(dep_ref, g * 2 + j, rows, total_rows)
        for off in (-2, 2, 6, 10):

            @pl.when(offset == off)
            def _(j=j, off=off):
                def move(i, carry):
                    cs = pl.ds(i * 4, 4)
                    t8[j, cs] = cut(tbuf[slot, j, cs].astype(jnp.float32), off)
                    w8[j, cs] = cut(wbuf[slot, j, cs].astype(jnp.float32), off)
                    return carry

                lax.fori_loop(0, width // 4, move, 0)

    def interleave(a, b, ks):
        sub = lax.broadcasted_iota(jnp.int32, a.shape, a.ndim - 2)
        b = pltpu.roll(b, 4, a.ndim - 2)
        for k in ks:
            e = jnp.where((sub + 8 - k) % 8 < 4, a, b)
            yield k, (pltpu.roll(e, 8 - k, a.ndim - 2) if k else e)

    def build(i, carry):
        for u in range(2):
            col = i * 2 + u
            for k, value in interleave(t8[0, col], t8[1, col], range(5)):
                s_ref[k, col] = value
        return carry

    lax.fori_loop(0, width // 2, build, 0)

    def packed_ext(j, col):
        low = w8[j, col]
        high = w8[j, col + half]
        lane = lax.broadcasted_iota(jnp.int32, low.shape, 1)
        return jnp.where(
            lane < 64, 2.0 * low - pltpu.roll(low, 64, 1), 2.0 * pltpu.roll(high, 64, 1) - high
        )

    def build_winds(i, carry):
        for u in range(2):
            col = 1 + i * 2 + u
            for k, value in interleave(packed_ext(0, col), packed_ext(1, col), range(1, 4)):
                p_ref[k - 1, col] = value
        return carry

    lax.fori_loop(0, (half + 2) // 2, build_winds, 0)

    block = 8

    def trace(i, carry):
        first = i * block
        low = here_ref[pl.ds(first, block)].astype(jnp.float32)
        high = here_ref[pl.ds(first + half, block)].astype(jnp.float32)
        lane = lax.broadcasted_iota(jnp.int32, low.shape, 2)
        east = (lane % 64) < 32
        here = jnp.where(lane < 64, low, pltpu.roll(high, 64, 2))
        d = jnp.clip(here, -CLIP_BOUND, CLIP_BOUND)
        for _ in range(TRAJ):
            swapped = jnp.where(east, pltpu.roll(d, 96, 2), pltpu.roll(d, 32, 2))
            lon = linear_near(jnp.where(east, d, swapped))
            lat = linear_near(jnp.where(east, swapped, d))
            acc = None
            for b in range(3):
                line = None
                for a in range(3):
                    term = lon[a] * p_ref[b, pl.ds(first + 1 + a, block)]
                    line = term if line is None else line + term
                line = lat[b] * line
                acc = line if acc is None else acc + line
            d = jnp.clip(0.5 * (here + acc), -CLIP_BOUND, CLIP_BOUND)
        hi = d.astype(jnp.bfloat16).astype(jnp.float32)
        d_ref[pl.ds(first, block), :, :128] = hi
        d_ref[pl.ds(first, block), :, 128:] = d - hi
        return carry

    lax.fori_loop(0, half // block, trace, 0)

    both = d_ref[...].reshape(half * 8, 256).astype(jnp.bfloat16)
    for part in range(4):
        at = slice(part * tracer_ch, (part + 1) * tracer_ch)
        r_ref[:, :, at] = jnp.dot(
            both, e_ref[:, at], preferred_element_type=jnp.float32
        ).reshape(half, 8, tracer_ch)

    def interpolate(i, carry):
        for h in range(2):
            for v in range(lane_tiles):
                lanes = slice(v * 128, (v + 1) * 128)
                re = r_ref[i, :, (2 * h) * tracer_ch + v * 128 : (2 * h) * tracer_ch + (v + 1) * 128]
                rn = r_ref[i, :, (2 * h + 1) * tracer_ch + v * 128 : (2 * h + 1) * tracer_ch + (v + 1) * 128]
                cubic = cubic_all(re)
                linear = [linear_kernel(re - 2.0)] + linear_near(re) + [linear_kernel(re + 2.0)]
                lat = cubic_all(rn)
                inner = {-1: rn > 0.0, 1: rn < 0.0}
                acc = None
                for b in range(-2, 3):
                    line = None
                    for a in range(5):
                        if b == 0:
                            weight = cubic[a]
                        elif abs(b) == 2:
                            weight = linear[a]
                        else:
                            weight = jnp.where(inner[b], cubic[a], linear[a])
                        term = weight * s_ref[b + 2, i + half * h + a, :, lanes]
                        line = term if line is None else line + term
                    line = lat[b + 2] * line
                    acc = line if acc is None else acc + line
                out_ref[i + half * h, :, lanes] = acc.astype(out_ref.dtype)
        return carry

    lax.fori_loop(0, half, interpolate, 0)


def advect(tracers_shape, wind_fields, departures, wt, ww):
    columns, total_rows, tracer_ch = tracers_shape
    levels = wind_fields.shape[-1] // 4
    bands = departures.shape[1]
    rows = total_rows // bands
    width = columns + 4
    half = columns // 2
    f32 = jnp.float32
    return pl.pallas_call(
        functools.partial(advect_kernel, columns, rows, levels),
        out_shape=jax.ShapeDtypeStruct(tracers_shape, jnp.bfloat16),
        grid_spec=pltpu.PrefetchScalarGridSpec(
            num_scalar_prefetch=1,
            grid=(bands // 2,),
            in_specs=[
                pl.BlockSpec((columns, 8, 4 * levels), lambda g, dep: (0, g, 0)),
                pl.BlockSpec(memory_space=pl.ANY),
                pl.BlockSpec(memory_space=pl.ANY),
            ],
            out_specs=pl.BlockSpec((columns, 8, tracer_ch), lambda g, dep: (0, g, 0)),
            scratch_shapes=[
                pltpu.VMEM((2, 2, width, 16, tracer_ch), jnp.bfloat16),
                pltpu.VMEM((2, 2, width, 16, 4 * levels), jnp.bfloat16),
                pltpu.VMEM((2, width, 8, tracer_ch), f32),
                pltpu.VMEM((2, width, 8, 4 * levels), f32),
                pltpu.VMEM((5, width, 8, tracer_ch), f32),
                pltpu.VMEM((3, half + 4, 8, 4 * levels), f32),
                pltpu.VMEM((half, 8, 4 * tracer_ch), f32),
                pltpu.VMEM((half, 8, 256), f32),
                pltpu.VMEM((256, 4 * tracer_ch), jnp.bfloat16),
                pltpu.SemaphoreType.DMA((2, 2, 2)),
            ],
        ),
        compiler_params=pltpu.CompilerParams(vmem_limit_bytes=40 * 1024 * 1024),
        name="advect",
    )(departures[0], wind_fields, wt, ww)

def shifted(block, distance):
    count = lax.axis_size("lon")
    route = [((i - distance) % count, i) for i in range(count)]
    return lax.ppermute(block, "lon", route)


def window(block):
    pieces = [shifted(block[-2:], -LOW + 1)]
    for offset in range(LOW, HIGH + 1):
        pieces.append(block if offset == 0 else shifted(block, -offset))
    pieces.append(shifted(block[:2], -HIGH - 1))
    return jnp.concatenate(pieces, 0)


def on_device(tracers, wind_fields, departures):
    return advect(tracers.shape, wind_fields, departures, window(tracers), window(wind_fields))


def solution(mesh):
    placed = P(("groups", "lon"), None, None)
    return jax.shard_map(
        on_device,
        mesh=mesh,
        in_specs=(placed, placed, placed),
        out_specs=placed,
        check_vma=False,
    )
```

```python
import functools

import jax
import jax.numpy as jnp
from jax import lax
from jax.experimental import pallas as pl
from jax.experimental.pallas import tpu as pltpu
from jax.sharding import PartitionSpec as P

CAP = 4
TRAJ = 3
CLIP_BOUND = 0.95
LOW, HIGH = -3, 4
CHUNKS = 8
MESH = pl.DeviceIdType.MESH


def linear_kernel(distance):
    return jnp.maximum(1.0 - jnp.abs(distance), 0.0)


def linear_near(r):
    return [jnp.maximum(r, 0.0), 1.0 - jnp.abs(r), jnp.maximum(-r, 0.0)]


def cubic_all(r):
    t = jnp.abs(r)
    u = 1.0 - t
    v = 1.0 + t
    w = 2.0 - t
    uw = u * w
    tv = t * v
    near0 = 0.5 * (uw * v)
    near1 = 0.5 * (tv * w)
    far1 = (-1.0 / 6.0) * (uw * t)
    far2 = (-1.0 / 6.0) * (tv * u)
    pos = r > 0.0
    zero = jnp.zeros_like(t)
    return [
        jnp.where(pos, far2, zero),
        jnp.where(pos, near1, far1),
        near0,
        jnp.where(pos, far1, near1),
        jnp.where(pos, zero, far2),
    ]


def place(dep_ref, band, rows, total_rows):
    source = band - dep_ref[band, 1]
    first = source * rows - 2
    base = jnp.clip((first + 8) // 8 * 8 - 8, 0, total_rows - 16)
    return base, first - base


def advect_kernel(columns, rows, levels, dep_ref, here_ref, wt_ref, ww_ref, out_ref,
                  tbuf, wbuf, t8, w8, s_ref, p_ref, r_ref, d_ref, e_ref, sems):
    g = pl.program_id(0)
    steps = pl.num_programs(0)
    total_rows = wt_ref.shape[1]
    width = columns + 4
    tracer_ch = wt_ref.shape[2]
    lane_tiles = tracer_ch // 128
    half = columns // 2
    slot = lax.rem(g, 2)

    def copies(step, where, j):
        band = step * 2 + j
        base, _ = place(dep_ref, band, rows, total_rows)
        start = (HIGH - 1 - dep_ref[band, 0]) * columns
        at = (pl.ds(start, width), pl.ds(pl.multiple_of(base, 8), 16), slice(None))
        return (
            pltpu.make_async_copy(wt_ref.at[at], tbuf.at[where, j], sems.at[where, j, 0]),
            pltpu.make_async_copy(ww_ref.at[at], wbuf.at[where, j], sems.at[where, j, 1]),
        )

    @pl.when(g == 0)
    def _():
        for j in range(2):
            for c in copies(0, 0, j):
                c.start()
        row = lax.broadcasted_iota(jnp.int32, e_ref.shape, 0)
        col = lax.broadcasted_iota(jnp.int32, e_ref.shape, 1)
        part = col // tracer_ch
        level = (col % tracer_ch) // (tracer_ch // levels)
        hit = (row % 128) == part * levels + level
        e_ref[...] = jnp.where(hit, 1.0, 0.0).astype(e_ref.dtype)

    @pl.when(g + 1 < steps)
    def _():
        for j in range(2):
            for c in copies(g + 1, 1 - slot, j):
                c.start()

    for j in range(2):
        for c in copies(g, slot, j):
            c.wait()

    def cut(x, off):
        if off < 0:
            return jnp.concatenate([x[:, :1]] * (-off) + [x[:, : 8 + off]], axis=1)
        if off + 8 > 16:
            return jnp.concatenate([x[:, off:]] + [x[:, 15:]] * (off - 8), axis=1)
        return x[:, off : off + 8]

    for j in range(2):
        _, offset = place(dep_ref, g * 2 + j, rows, total_rows)
        for off in (-2, 2, 6, 10):

            @pl.when(offset == off)
            def _(j=j, off=off):
                def move(i, carry):
                    cs = pl.ds(i * 4, 4)
                    t8[j, cs] = cut(tbuf[slot, j, cs].astype(jnp.float32), off)
                    w8[j, cs] = cut(wbuf[slot, j, cs].astype(jnp.float32), off)
                    return carry

                lax.fori_loop(0, width // 4, move, 0)

    def interleave(a, b, ks):
        sub = lax.broadcasted_iota(jnp.int32, a.shape, a.ndim - 2)
        b = pltpu.roll(b, 4, a.ndim - 2)
        for k in ks:
            e = jnp.where((sub + 8 - k) % 8 < 4, a, b)
            yield k, (pltpu.roll(e, 8 - k, a.ndim - 2) if k else e)

    def build(i, carry):
        for u in range(2):
            col = i * 2 + u
            for k, value in interleave(t8[0, col], t8[1, col], range(5)):
                s_ref[k, col] = value
        return carry

    lax.fori_loop(0, width // 2, build, 0)

    def packed_ext(j, col):
        low = w8[j, col]
        high = w8[j, col + half]
        lane = lax.broadcasted_iota(jnp.int32, low.shape, 1)
        return jnp.where(
            lane < 64, 2.0 * low - pltpu.roll(low, 64, 1), 2.0 * pltpu.roll(high, 64, 1) - high
        )

    def build_winds(i, carry):
        for u in range(2):
            col = 1 + i * 2 + u
            for k, value in interleave(packed_ext(0, col), packed_ext(1, col), range(1, 4)):
                p_ref[k - 1, col] = value
        return carry

    lax.fori_loop(0, (half + 2) // 2, build_winds, 0)

    block = 8

    def trace(i, carry):
        first = i * block
        low = here_ref[pl.ds(first, block)].astype(jnp.float32)
        high = here_ref[pl.ds(first + half, block)].astype(jnp.float32)
        lane = lax.broadcasted_iota(jnp.int32, low.shape, 2)
        east = (lane % 64) < 32
        here = jnp.where(lane < 64, low, pltpu.roll(high, 64, 2))
        d = jnp.clip(here, -CLIP_BOUND, CLIP_BOUND)
        for _ in range(TRAJ):
            swapped = jnp.where(east, pltpu.roll(d, 96, 2), pltpu.roll(d, 32, 2))
            lon = linear_near(jnp.where(east, d, swapped))
            lat = linear_near(jnp.where(east, swapped, d))
            acc = None
            for b in range(3):
                line = None
                for a in range(3):
                    term = lon[a] * p_ref[b, pl.ds(first + 1 + a, block)]
                    line = term if line is None else line + term
                line = lat[b] * line
                acc = line if acc is None else acc + line
            d = jnp.clip(0.5 * (here + acc), -CLIP_BOUND, CLIP_BOUND)
        hi = d.astype(jnp.bfloat16).astype(jnp.float32)
        d_ref[pl.ds(first, block), :, :128] = hi
        d_ref[pl.ds(first, block), :, 128:] = d - hi
        return carry

    lax.fori_loop(0, half // block, trace, 0)

    both = d_ref[...].reshape(half * 8, 256).astype(jnp.bfloat16)
    for part in range(4):
        at = slice(part * tracer_ch, (part + 1) * tracer_ch)
        r_ref[:, :, at] = jnp.dot(
            both, e_ref[:, at], preferred_element_type=jnp.float32
        ).reshape(half, 8, tracer_ch)

    def interpolate(i, carry):
        for h in range(2):
            for v in range(lane_tiles):
                lanes = slice(v * 128, (v + 1) * 128)
                re = r_ref[i, :, (2 * h) * tracer_ch + v * 128 : (2 * h) * tracer_ch + (v + 1) * 128]
                rn = r_ref[i, :, (2 * h + 1) * tracer_ch + v * 128 : (2 * h + 1) * tracer_ch + (v + 1) * 128]
                cubic = cubic_all(re)
                linear = [linear_kernel(re - 2.0)] + linear_near(re) + [linear_kernel(re + 2.0)]
                lat = cubic_all(rn)
                inner = {-1: rn > 0.0, 1: rn < 0.0}
                acc = None
                for b in range(-2, 3):
                    line = None
                    for a in range(5):
                        if b == 0:
                            weight = cubic[a]
                        elif abs(b) == 2:
                            weight = linear[a]
                        else:
                            weight = jnp.where(inner[b], cubic[a], linear[a])
                        term = weight * s_ref[b + 2, i + half * h + a, :, lanes]
                        line = term if line is None else line + term
                    line = lat[b + 2] * line
                    acc = line if acc is None else acc + line
                out_ref[i + half * h, :, lanes] = acc.astype(out_ref.dtype)
        return carry

    lax.fori_loop(0, half, interpolate, 0)


def advect(tracers_shape, wind_fields, departures, wt, ww):
    columns, total_rows, tracer_ch = tracers_shape
    levels = wind_fields.shape[-1] // 4
    bands = departures.shape[1]
    rows = total_rows // bands
    width = columns + 4
    half = columns // 2
    f32 = jnp.float32
    return pl.pallas_call(
        functools.partial(advect_kernel, columns, rows, levels),
        out_shape=jax.ShapeDtypeStruct(tracers_shape, jnp.bfloat16),
        grid_spec=pltpu.PrefetchScalarGridSpec(
            num_scalar_prefetch=1,
            grid=(bands // 2,),
            in_specs=[
                pl.BlockSpec((columns, 8, 4 * levels), lambda g, dep: (0, g, 0)),
                pl.BlockSpec(memory_space=pl.ANY),
                pl.BlockSpec(memory_space=pl.ANY),
            ],
            out_specs=pl.BlockSpec((columns, 8, tracer_ch), lambda g, dep: (0, g, 0)),
            scratch_shapes=[
                pltpu.VMEM((2, 2, width, 16, tracer_ch), jnp.bfloat16),
                pltpu.VMEM((2, 2, width, 16, 4 * levels), jnp.bfloat16),
                pltpu.VMEM((2, width, 8, tracer_ch), f32),
                pltpu.VMEM((2, width, 8, 4 * levels), f32),
                pltpu.VMEM((5, width, 8, tracer_ch), f32),
                pltpu.VMEM((3, half + 4, 8, 4 * levels), f32),
                pltpu.VMEM((half, 8, 4 * tracer_ch), f32),
                pltpu.VMEM((half, 8, 256), f32),
                pltpu.VMEM((256, 4 * tracer_ch), jnp.bfloat16),
                pltpu.SemaphoreType.DMA((2, 2, 2)),
            ],
        ),
        compiler_params=pltpu.CompilerParams(vmem_limit_bytes=40 * 1024 * 1024),
        name="advect",
    )(departures[0], wind_fields, wt, ww)

def gather_kernel(columns, chunks, t_ref, w_ref, wt_ref, ww_ref, send, recv, edge_send, edge_recv, keep):
    count = lax.axis_size("lon")
    me = lax.axis_index("lon")
    core = lax.rem(me, 2)
    odd = lax.rem(me // 2, 2)
    piece = columns // chunks
    pairs = ((t_ref, wt_ref), (w_ref, ww_ref))

    def device(distance):
        return lax.rem(me + distance + count, count)

    def landing(offset, q):
        return pl.ds(2 + (offset - LOW) * columns + q * piece, piece)

    def own(flow, q, distance):
        return [
            pltpu.make_async_remote_copy(
                src_ref=local.at[pl.ds(q * piece, piece)],
                dst_ref=far.at[landing(-distance, q)],
                send_sem=send.at[flow, q, a],
                recv_sem=recv.at[-distance - LOW, q, a],
                device_id={"lon": device(distance)},
                device_id_type=MESH,
            )
            for a, (local, far) in enumerate(pairs)
        ]

    def relay(flow, q, offset, distance):
        return [
            pltpu.make_async_remote_copy(
                src_ref=far.at[landing(offset, q)],
                dst_ref=far.at[landing(offset - distance, q)],
                send_sem=send.at[flow, q, a],
                recv_sem=recv.at[offset - distance - LOW, q, a],
                device_id={"lon": device(distance)},
                device_id_type=MESH,
            )
            for a, (_, far) in enumerate(pairs)
        ]

    def arrived(offset, q):
        for a, (local, far) in enumerate(pairs):
            pltpu.make_async_remote_copy(
                src_ref=local.at[pl.ds(0, piece)],
                dst_ref=far.at[landing(offset, q)],
                send_sem=send.at[0, q, a],
                recv_sem=recv.at[offset - LOW, q, a],
                device_id={"lon": device(1)},
                device_id_type=MESH,
            ).wait_recv()

    def edges():
        out = []
        for a, (local, far) in enumerate(pairs):
            size = (HIGH - LOW + 1) * columns
            for side, (source, target, distance) in enumerate(
                ((columns - 2, 0, 1 - LOW), (0, 2 + size, -1 - HIGH))
            ):
                out.append(
                    pltpu.make_async_remote_copy(
                        src_ref=local.at[pl.ds(source, 2)],
                        dst_ref=far.at[pl.ds(target, 2)],
                        send_sem=edge_send.at[side, a],
                        recv_sem=edge_recv.at[side, a],
                        device_id={"lon": device(distance)},
                        device_id_type=MESH,
                    )
                )
        return out

    def stay():
        return [
            pltpu.make_async_copy(local, far.at[pl.ds(2 - LOW * columns, columns)], keep.at[a])
            for a, (local, far) in enumerate(pairs)
        ]

    sibling = 1 - 2 * core
    across = 2 - 4 * odd

    barrier = pltpu.get_barrier_semaphore()
    reach = 1 + HIGH
    for distance in range(1, reach + 1):
        for way in (distance, -distance):
            pl.semaphore_signal(
                barrier, inc=1, device_id={"lon": device(way)}, device_id_type=MESH
            )
    pl.semaphore_wait(barrier, 2 * reach)

    def begin(copies):
        for c in copies:
            c.start()

    def end(copies):
        for c in copies:
            c.wait_send()

    passes_on = (1 - odd) + odd * core

    def first(q, carry):
        begin(own(1, q, across))
        begin(own(2, q, -4))

        @pl.when(core == 1)
        def _():
            begin(own(3, q, 3))

        begin(own(0, q, sibling))
        return carry

    lax.fori_loop(0, chunks, first, 0)
    begin(edges())
    begin(stay())

    def late(q):
        arrived(-across, q)
        begin(relay(7, q, -across, sibling))

    def step(q, carry):
        arrived(across, q)

        @pl.when(passes_on == 1)
        def _():
            begin(relay(4, q, across, 2 * across))

        begin(relay(5, q, across, sibling))
        arrived(4, q)

        @pl.when(core == 0)
        def _():
            @pl.when(odd == 0)
            def _():
                begin(relay(8, q, 4, 2))

            begin(relay(6, q, 4, sibling))

        @pl.when(q > 0)
        def _():
            late(q - 1)

        return carry

    lax.fori_loop(0, chunks, step, 0)
    late(chunks - 1)

    def finish(q, carry):
        for offset in (-3, -1, 1, 3):
            arrived(offset, q)
        end(own(0, q, sibling))
        end(own(1, q, across))
        end(own(2, q, -4))

        @pl.when(core == 1)
        def _():
            end(own(3, q, 3))

        @pl.when(passes_on == 1)
        def _():
            end(relay(4, q, across, 2 * across))

        end(relay(5, q, across, sibling))

        @pl.when(core == 0)
        def _():
            @pl.when(odd == 0)
            def _():
                end(relay(8, q, 4, 2))

            end(relay(6, q, 4, sibling))

        end(relay(7, q, -across, sibling))
        return carry

    lax.fori_loop(0, chunks, finish, 0)
    for c in edges():
        c.wait()
    for c in stay():
        c.wait()


def gather_window(tracers, wind_fields):
    columns = tracers.shape[0]
    long = (HIGH - LOW + 1) * columns + 4
    shapes = [jax.ShapeDtypeStruct((long,) + x.shape[1:], x.dtype) for x in (tracers, wind_fields)]
    dma = pltpu.SemaphoreType.DMA
    return pl.pallas_call(
        functools.partial(gather_kernel, columns, CHUNKS),
        out_shape=shapes,
        in_specs=[pl.BlockSpec(memory_space=pl.ANY)] * 2,
        out_specs=[pl.BlockSpec(memory_space=pl.ANY)] * 2,
        scratch_shapes=[
            dma((9, CHUNKS, 2)),
            dma((HIGH - LOW + 1, CHUNKS, 2)),
            dma((2, 2)),
            dma((2, 2)),
            dma((2,)),
        ],
        compiler_params=pltpu.CompilerParams(
            collective_id=0, has_side_effects=True, vmem_limit_bytes=1024 * 1024
        ),
        name="gather_window",
    )(tracers, wind_fields)


def on_device(tracers, wind_fields, departures):
    wt, ww = gather_window(tracers, wind_fields)
    return advect(tracers.shape, wind_fields, departures, wt, ww)


def solution(mesh):
    placed = P(("groups", "lon"), None, None)
    return jax.shard_map(
        on_device,
        mesh=mesh,
        in_specs=(placed, placed, placed),
        out_specs=placed,
        check_vma=False,
    )
```

```python
import functools

import jax
import jax.numpy as jnp
from jax import lax
from jax.experimental import pallas as pl
from jax.experimental.pallas import tpu as pltpu
from jax.sharding import PartitionSpec as P

CAP = 4
TRAJ = 3
CLIP_BOUND = 0.95
LOW, HIGH = -3, 4
CHUNKS = 8
MESH = pl.DeviceIdType.MESH


def linear_kernel(distance):
    return jnp.maximum(1.0 - jnp.abs(distance), 0.0)


def linear_near(r):
    return [jnp.maximum(r, 0.0), 1.0 - jnp.abs(r), jnp.maximum(-r, 0.0)]


def cubic_all(r):
    t = jnp.abs(r)
    u = 1.0 - t
    v = 1.0 + t
    w = 2.0 - t
    uw = u * w
    tv = t * v
    near0 = 0.5 * (uw * v)
    near1 = 0.5 * (tv * w)
    far1 = (-1.0 / 6.0) * (uw * t)
    far2 = (-1.0 / 6.0) * (tv * u)
    pos = r > 0.0
    zero = jnp.zeros_like(t)
    return [
        jnp.where(pos, far2, zero),
        jnp.where(pos, near1, far1),
        near0,
        jnp.where(pos, far1, near1),
        jnp.where(pos, zero, far2),
    ]


def place(dep_ref, band, rows, total_rows):
    source = band - dep_ref[band, 1]
    first = source * rows - 2
    base = jnp.clip((first + 8) // 8 * 8 - 8, 0, total_rows - 16)
    return base, first - base


def advect_kernel(columns, rows, levels, dep_ref, here_ref, wt_ref, ww_ref, out_ref,
                  tbuf, wbuf, t8, w8, s_ref, p_ref, r_ref, d_ref, e_ref, sems):
    g = pl.program_id(0)
    steps = pl.num_programs(0)
    total_rows = wt_ref.shape[1]
    width = columns + 4
    tracer_ch = wt_ref.shape[2]
    lane_tiles = tracer_ch // 128
    half = columns // 2
    slot = lax.rem(g, 2)

    def copies(step, where, j):
        band = step * 2 + j
        base, _ = place(dep_ref, band, rows, total_rows)
        start = (HIGH - 1 - dep_ref[band, 0]) * columns
        at = (pl.ds(start, width), pl.ds(pl.multiple_of(base, 8), 16), slice(None))
        return (
            pltpu.make_async_copy(wt_ref.at[at], tbuf.at[where, j], sems.at[where, j, 0]),
            pltpu.make_async_copy(ww_ref.at[at], wbuf.at[where, j], sems.at[where, j, 1]),
        )

    @pl.when(g == 0)
    def _():
        for j in range(2):
            for c in copies(0, 0, j):
                c.start()
        row = lax.broadcasted_iota(jnp.int32, e_ref.shape, 0)
        col = lax.broadcasted_iota(jnp.int32, e_ref.shape, 1)
        part = col // tracer_ch
        level = (col % tracer_ch) // (tracer_ch // levels)
        hit = (row % 128) == part * levels + level
        e_ref[...] = jnp.where(hit, 1.0, 0.0).astype(e_ref.dtype)

    @pl.when(g + 1 < steps)
    def _():
        for j in range(2):
            for c in copies(g + 1, 1 - slot, j):
                c.start()

    for j in range(2):
        for c in copies(g, slot, j):
            c.wait()

    def cut(x, off):
        if off < 0:
            return jnp.concatenate([x[:, :1]] * (-off) + [x[:, : 8 + off]], axis=1)
        if off + 8 > 16:
            return jnp.concatenate([x[:, off:]] + [x[:, 15:]] * (off - 8), axis=1)
        return x[:, off : off + 8]

    for j in range(2):
        _, offset = place(dep_ref, g * 2 + j, rows, total_rows)
        for off in (-2, 2, 6, 10):

            @pl.when(offset == off)
            def _(j=j, off=off):
                def move(i, carry):
                    cs = pl.ds(i * 4, 4)
                    t8[j, cs] = cut(tbuf[slot, j, cs].astype(jnp.float32), off)
                    w8[j, cs] = cut(wbuf[slot, j, cs].astype(jnp.float32), off)
                    return carry

                lax.fori_loop(0, width // 4, move, 0)

    def interleave(a, b, ks):
        sub = lax.broadcasted_iota(jnp.int32, a.shape, a.ndim - 2)
        b = pltpu.roll(b, 4, a.ndim - 2)
        for k in ks:
            e = jnp.where((sub + 8 - k) % 8 < 4, a, b)
            yield k, (pltpu.roll(e, 8 - k, a.ndim - 2) if k else e)

    def build(i, carry):
        for u in range(2):
            col = i * 2 + u
            for k, value in interleave(t8[0, col], t8[1, col], range(5)):
                s_ref[k, col] = value
        return carry

    lax.fori_loop(0, width // 2, build, 0)

    def packed_ext(j, col):
        low = w8[j, col]
        high = w8[j, col + half]
        lane = lax.broadcasted_iota(jnp.int32, low.shape, 1)
        return jnp.where(
            lane < 64, 2.0 * low - pltpu.roll(low, 64, 1), 2.0 * pltpu.roll(high, 64, 1) - high
        )

    def build_winds(i, carry):
        for u in range(2):
            col = 1 + i * 2 + u
            for k, value in interleave(packed_ext(0, col), packed_ext(1, col), range(1, 4)):
                p_ref[k - 1, col] = value
        return carry

    lax.fori_loop(0, (half + 2) // 2, build_winds, 0)

    block = 8

    def trace(i, carry):
        first = i * block
        low = here_ref[pl.ds(first, block)].astype(jnp.float32)
        high = here_ref[pl.ds(first + half, block)].astype(jnp.float32)
        lane = lax.broadcasted_iota(jnp.int32, low.shape, 2)
        east = (lane % 64) < 32
        here = jnp.where(lane < 64, low, pltpu.roll(high, 64, 2))
        d = jnp.clip(here, -CLIP_BOUND, CLIP_BOUND)
        for _ in range(TRAJ):
            swapped = jnp.where(east, pltpu.roll(d, 96, 2), pltpu.roll(d, 32, 2))
            lon = linear_near(jnp.where(east, d, swapped))
            lat = linear_near(jnp.where(east, swapped, d))
            acc = None
            for b in range(3):
                line = None
                for a in range(3):
                    term = lon[a] * p_ref[b, pl.ds(first + 1 + a, block)]
                    line = term if line is None else line + term
                line = lat[b] * line
                acc = line if acc is None else acc + line
            d = jnp.clip(0.5 * (here + acc), -CLIP_BOUND, CLIP_BOUND)
        hi = d.astype(jnp.bfloat16).astype(jnp.float32)
        d_ref[pl.ds(first, block), :, :128] = hi
        d_ref[pl.ds(first, block), :, 128:] = d - hi
        return carry

    lax.fori_loop(0, half // block, trace, 0)

    both = d_ref[...].reshape(half * 8, 256).astype(jnp.bfloat16)
    for part in range(4):
        at = slice(part * tracer_ch, (part + 1) * tracer_ch)
        r_ref[:, :, at] = jnp.dot(
            both, e_ref[:, at], preferred_element_type=jnp.float32
        ).reshape(half, 8, tracer_ch)

    def interpolate(i, carry):
        for h in range(2):
            for v in range(lane_tiles):
                lanes = slice(v * 128, (v + 1) * 128)
                re = r_ref[i, :, (2 * h) * tracer_ch + v * 128 : (2 * h) * tracer_ch + (v + 1) * 128]
                rn = r_ref[i, :, (2 * h + 1) * tracer_ch + v * 128 : (2 * h + 1) * tracer_ch + (v + 1) * 128]
                cubic = cubic_all(re)
                linear = [linear_kernel(re - 2.0)] + linear_near(re) + [linear_kernel(re + 2.0)]
                lat = cubic_all(rn)
                inner = {-1: rn > 0.0, 1: rn < 0.0}
                acc = None
                for b in range(-2, 3):
                    line = None
                    for a in range(5):
                        if b == 0:
                            weight = cubic[a]
                        elif abs(b) == 2:
                            weight = linear[a]
                        else:
                            weight = jnp.where(inner[b], cubic[a], linear[a])
                        term = weight * s_ref[b + 2, i + half * h + a, :, lanes]
                        line = term if line is None else line + term
                    line = lat[b + 2] * line
                    acc = line if acc is None else acc + line
                out_ref[i + half * h, :, lanes] = acc.astype(out_ref.dtype)
        return carry

    lax.fori_loop(0, half, interpolate, 0)


def advect(tracers_shape, wind_fields, departures, wt, ww):
    columns, total_rows, tracer_ch = tracers_shape
    levels = wind_fields.shape[-1] // 4
    bands = departures.shape[1]
    rows = total_rows // bands
    width = columns + 4
    half = columns // 2
    f32 = jnp.float32
    return pl.pallas_call(
        functools.partial(advect_kernel, columns, rows, levels),
        out_shape=jax.ShapeDtypeStruct(tracers_shape, jnp.bfloat16),
        grid_spec=pltpu.PrefetchScalarGridSpec(
            num_scalar_prefetch=1,
            grid=(bands // 2,),
            in_specs=[
                pl.BlockSpec((columns, 8, 4 * levels), lambda g, dep: (0, g, 0)),
                pl.BlockSpec(memory_space=pl.ANY),
                pl.BlockSpec(memory_space=pl.ANY),
            ],
            out_specs=pl.BlockSpec((columns, 8, tracer_ch), lambda g, dep: (0, g, 0)),
            scratch_shapes=[
                pltpu.VMEM((2, 2, width, 16, tracer_ch), jnp.bfloat16),
                pltpu.VMEM((2, 2, width, 16, 4 * levels), jnp.bfloat16),
                pltpu.VMEM((2, width, 8, tracer_ch), f32),
                pltpu.VMEM((2, width, 8, 4 * levels), f32),
                pltpu.VMEM((5, width, 8, tracer_ch), f32),
                pltpu.VMEM((3, half + 4, 8, 4 * levels), f32),
                pltpu.VMEM((half, 8, 4 * tracer_ch), f32),
                pltpu.VMEM((half, 8, 256), f32),
                pltpu.VMEM((256, 4 * tracer_ch), jnp.bfloat16),
                pltpu.SemaphoreType.DMA((2, 2, 2)),
            ],
        ),
        compiler_params=pltpu.CompilerParams(vmem_limit_bytes=60 * 1024 * 1024),
        name="advect",
    )(departures[0], wind_fields, wt, ww)

def gather_kernel(columns, chunks, t_ref, w_ref, wt_ref, ww_ref, send, recv, edge_send, edge_recv, keep):
    count = lax.axis_size("lon")
    me = lax.axis_index("lon")
    core = lax.rem(me, 2)
    odd = lax.rem(me // 2, 2)
    piece = columns // chunks
    pairs = ((t_ref, wt_ref), (w_ref, ww_ref))

    def device(distance):
        return lax.rem(me + distance + count, count)

    def landing(offset, q):
        return pl.ds(2 + (offset - LOW) * columns + q * piece, piece)

    def own(flow, q, distance):
        return [
            pltpu.make_async_remote_copy(
                src_ref=local.at[pl.ds(q * piece, piece)],
                dst_ref=far.at[landing(-distance, q)],
                send_sem=send.at[flow, q, a],
                recv_sem=recv.at[-distance - LOW, q, a],
                device_id={"lon": device(distance)},
                device_id_type=MESH,
            )
            for a, (local, far) in enumerate(pairs)
        ]

    def relay(flow, q, offset, distance):
        return [
            pltpu.make_async_remote_copy(
                src_ref=far.at[landing(offset, q)],
                dst_ref=far.at[landing(offset - distance, q)],
                send_sem=send.at[flow, q, a],
                recv_sem=recv.at[offset - distance - LOW, q, a],
                device_id={"lon": device(distance)},
                device_id_type=MESH,
            )
            for a, (_, far) in enumerate(pairs)
        ]

    def arrived(offset, q):
        for a, (local, far) in enumerate(pairs):
            pltpu.make_async_remote_copy(
                src_ref=local.at[pl.ds(0, piece)],
                dst_ref=far.at[landing(offset, q)],
                send_sem=send.at[0, q, a],
                recv_sem=recv.at[offset - LOW, q, a],
                device_id={"lon": device(1)},
                device_id_type=MESH,
            ).wait_recv()

    def edges():
        out = []
        for a, (local, far) in enumerate(pairs):
            size = (HIGH - LOW + 1) * columns
            for side, (source, target, distance) in enumerate(
                ((columns - 2, 0, 1 - LOW), (0, 2 + size, -1 - HIGH))
            ):
                out.append(
                    pltpu.make_async_remote_copy(
                        src_ref=local.at[pl.ds(source, 2)],
                        dst_ref=far.at[pl.ds(target, 2)],
                        send_sem=edge_send.at[side, a],
                        recv_sem=edge_recv.at[side, a],
                        device_id={"lon": device(distance)},
                        device_id_type=MESH,
                    )
                )
        return out

    def stay():
        return [
            pltpu.make_async_copy(local, far.at[pl.ds(2 - LOW * columns, columns)], keep.at[a])
            for a, (local, far) in enumerate(pairs)
        ]

    sibling = 1 - 2 * core
    across = 2 - 4 * odd

    barrier = pltpu.get_barrier_semaphore()
    reach = 1 + HIGH
    for distance in range(1, reach + 1):
        for way in (distance, -distance):
            pl.semaphore_signal(
                barrier, inc=1, device_id={"lon": device(way)}, device_id_type=MESH
            )
    pl.semaphore_wait(barrier, 2 * reach)

    def begin(copies):
        for c in copies:
            c.start()

    def end(copies):
        for c in copies:
            c.wait_send()

    passes_on = (1 - odd) * (1 - core)
    turns_back = odd * (1 - core)

    def first(q, carry):
        begin(own(1, q, across))
        begin(own(2, q, -4))

        @pl.when(core == 1)
        def _():
            begin(own(3, q, 3))

        begin(own(0, q, sibling))
        return carry

    lax.fori_loop(0, chunks, first, 0)
    begin(edges())
    begin(stay())

    def late(q):
        arrived(-across, q)
        begin(relay(7, q, -across, sibling))

    def step(q, carry):
        arrived(across, q)

        @pl.when(passes_on == 1)
        def _():
            begin(relay(4, q, across, 2 * across))

        begin(relay(5, q, across, sibling))
        arrived(4, q)

        @pl.when(odd == 0)
        def _():
            begin(relay(8, q, 4, 2))

        @pl.when(core == 0)
        def _():
            begin(relay(6, q, 4, sibling))

        @pl.when(turns_back == 1)
        def _():
            arrived(-3, q)
            begin(relay(3, q, -3, -1))

        @pl.when(q > 0)
        def _():
            late(q - 1)

        return carry

    lax.fori_loop(0, chunks, step, 0)
    late(chunks - 1)

    def finish(q, carry):
        for offset in (-1, 1, 3):
            arrived(offset, q)
        end(own(0, q, sibling))
        end(own(1, q, across))
        end(own(2, q, -4))

        @pl.when(core == 1)
        def _():
            end(own(3, q, 3))

        @pl.when(passes_on == 1)
        def _():
            end(relay(4, q, across, 2 * across))

        end(relay(5, q, across, sibling))

        @pl.when(odd == 0)
        def _():
            end(relay(8, q, 4, 2))

        @pl.when(core == 0)
        def _():
            end(relay(6, q, 4, sibling))

        @pl.when(turns_back == 1)
        def _():
            end(relay(3, q, -3, -1))

        @pl.when(turns_back == 0)
        def _():
            arrived(-3, q)

        end(relay(7, q, -across, sibling))
        return carry

    lax.fori_loop(0, chunks, finish, 0)
    for c in edges():
        c.wait()
    for c in stay():
        c.wait()


def gather_window(tracers, wind_fields):
    columns = tracers.shape[0]
    long = (HIGH - LOW + 1) * columns + 4
    shapes = [jax.ShapeDtypeStruct((long,) + x.shape[1:], x.dtype) for x in (tracers, wind_fields)]
    dma = pltpu.SemaphoreType.DMA
    return pl.pallas_call(
        functools.partial(gather_kernel, columns, CHUNKS),
        out_shape=shapes,
        in_specs=[pl.BlockSpec(memory_space=pl.ANY)] * 2,
        out_specs=[pl.BlockSpec(memory_space=pl.ANY)] * 2,
        scratch_shapes=[
            dma((9, CHUNKS, 2)),
            dma((HIGH - LOW + 1, CHUNKS, 2)),
            dma((2, 2)),
            dma((2, 2)),
            dma((2,)),
        ],
        compiler_params=pltpu.CompilerParams(collective_id=0, has_side_effects=True),
        name="gather_window",
    )(tracers, wind_fields)


def on_device(tracers, wind_fields, departures):
    wt, ww = gather_window(tracers, wind_fields)
    return advect(tracers.shape, wind_fields, departures, wt, ww)


def solution(mesh):
    placed = P(("groups", "lon"), None, None)
    return jax.shard_map(
        on_device,
        mesh=mesh,
        in_specs=(placed, placed, placed),
        out_specs=placed,
        check_vma=False,
    )
```

```python
import functools

import jax
import jax.numpy as jnp
from jax import lax
from jax.experimental import pallas as pl
from jax.experimental.pallas import tpu as pltpu
from jax.sharding import PartitionSpec as P

CAP = 4
TRAJ = 3
CLIP_BOUND = 0.95
LOW, HIGH = -3, 4
CHUNKS = 16
MESH = pl.DeviceIdType.MESH


def linear_kernel(distance):
    return jnp.maximum(1.0 - jnp.abs(distance), 0.0)


def linear_near(r):
    return [jnp.maximum(r, 0.0), 1.0 - jnp.abs(r), jnp.maximum(-r, 0.0)]


def cubic_all(r):
    t = jnp.abs(r)
    u = 1.0 - t
    v = 1.0 + t
    w = 2.0 - t
    uw = u * w
    tv = t * v
    near0 = 0.5 * (uw * v)
    near1 = 0.5 * (tv * w)
    far1 = (-1.0 / 6.0) * (uw * t)
    far2 = (-1.0 / 6.0) * (tv * u)
    pos = r > 0.0
    zero = jnp.zeros_like(t)
    return [
        jnp.where(pos, far2, zero),
        jnp.where(pos, near1, far1),
        near0,
        jnp.where(pos, far1, near1),
        jnp.where(pos, zero, far2),
    ]


def place(dep_ref, band, rows, total_rows):
    source = band - dep_ref[band, 1]
    first = source * rows - 2
    base = jnp.clip((first + 8) // 8 * 8 - 8, 0, total_rows - 16)
    return base, first - base


def advect_kernel(columns, rows, levels, dep_ref, here_ref, wt_ref, ww_ref, out_ref,
                  tbuf, wbuf, t8, w8, s_ref, p_ref, r_ref, d_ref, e_ref, sems):
    g = pl.program_id(0)
    steps = pl.num_programs(0)
    total_rows = wt_ref.shape[1]
    width = columns + 4
    tracer_ch = wt_ref.shape[2]
    lane_tiles = tracer_ch // 128
    half = columns // 2
    slot = lax.rem(g, 2)

    def copies(step, where, j):
        band = step * 2 + j
        base, _ = place(dep_ref, band, rows, total_rows)
        start = (HIGH - 1 - dep_ref[band, 0]) * columns
        at = (pl.ds(start, width), pl.ds(pl.multiple_of(base, 8), 16), slice(None))
        return (
            pltpu.make_async_copy(wt_ref.at[at], tbuf.at[where, j], sems.at[where, j, 0]),
            pltpu.make_async_copy(ww_ref.at[at], wbuf.at[where, j], sems.at[where, j, 1]),
        )

    @pl.when(g == 0)
    def _():
        for j in range(2):
            for c in copies(0, 0, j):
                c.start()
        row = lax.broadcasted_iota(jnp.int32, e_ref.shape, 0)
        col = lax.broadcasted_iota(jnp.int32, e_ref.shape, 1)
        part = col // tracer_ch
        level = (col % tracer_ch) // (tracer_ch // levels)
        hit = (row % 128) == part * levels + level
        e_ref[...] = jnp.where(hit, 1.0, 0.0).astype(e_ref.dtype)

    @pl.when(g + 1 < steps)
    def _():
        for j in range(2):
            for c in copies(g + 1, 1 - slot, j):
                c.start()

    for j in range(2):
        for c in copies(g, slot, j):
            c.wait()

    def cut(x, off):
        if off < 0:
            return jnp.concatenate([x[:, :1]] * (-off) + [x[:, : 8 + off]], axis=1)
        if off + 8 > 16:
            return jnp.concatenate([x[:, off:]] + [x[:, 15:]] * (off - 8), axis=1)
        return x[:, off : off + 8]

    for j in range(2):
        _, offset = place(dep_ref, g * 2 + j, rows, total_rows)
        for off in (-2, 2, 6, 10):

            @pl.when(offset == off)
            def _(j=j, off=off):
                def move(i, carry):
                    cs = pl.ds(i * 4, 4)
                    t8[j, cs] = cut(tbuf[slot, j, cs].astype(jnp.float32), off)
                    w8[j, cs] = cut(wbuf[slot, j, cs].astype(jnp.float32), off)
                    return carry

                lax.fori_loop(0, width // 4, move, 0)

    def interleave(a, b, ks):
        sub = lax.broadcasted_iota(jnp.int32, a.shape, a.ndim - 2)
        b = pltpu.roll(b, 4, a.ndim - 2)
        for k in ks:
            e = jnp.where((sub + 8 - k) % 8 < 4, a, b)
            yield k, (pltpu.roll(e, 8 - k, a.ndim - 2) if k else e)

    def build(i, carry):
        for u in range(4):
            col = i * 4 + u
            for k, value in interleave(t8[0, col], t8[1, col], range(5)):
                s_ref[k, col] = value
        return carry

    lax.fori_loop(0, width // 4, build, 0)

    def packed_ext(j, col):
        low = w8[j, col]
        high = w8[j, col + half]
        lane = lax.broadcasted_iota(jnp.int32, low.shape, 1)
        return jnp.where(
            lane < 64, 2.0 * low - pltpu.roll(low, 64, 1), 2.0 * pltpu.roll(high, 64, 1) - high
        )

    def build_winds(i, carry):
        for u in range(2):
            col = 1 + i * 2 + u
            for k, value in interleave(packed_ext(0, col), packed_ext(1, col), range(1, 4)):
                p_ref[k - 1, col] = value
        return carry

    lax.fori_loop(0, (half + 2) // 2, build_winds, 0)

    block = 8

    def trace(i, carry):
        first = i * block
        low = here_ref[pl.ds(first, block)].astype(jnp.float32)
        high = here_ref[pl.ds(first + half, block)].astype(jnp.float32)
        lane = lax.broadcasted_iota(jnp.int32, low.shape, 2)
        east = (lane % 64) < 32
        here = jnp.where(lane < 64, low, pltpu.roll(high, 64, 2))
        d = jnp.clip(here, -CLIP_BOUND, CLIP_BOUND)
        for _ in range(TRAJ):
            swapped = jnp.where(east, pltpu.roll(d, 96, 2), pltpu.roll(d, 32, 2))
            lon = linear_near(jnp.where(east, d, swapped))
            lat = linear_near(jnp.where(east, swapped, d))
            acc = None
            for b in range(3):
                line = None
                for a in range(3):
                    term = lon[a] * p_ref[b, pl.ds(first + 1 + a, block)]
                    line = term if line is None else line + term
                line = lat[b] * line
                acc = line if acc is None else acc + line
            d = jnp.clip(0.5 * (here + acc), -CLIP_BOUND, CLIP_BOUND)
        hi = d.astype(jnp.bfloat16).astype(jnp.float32)
        d_ref[pl.ds(first, block), :, :128] = hi
        d_ref[pl.ds(first, block), :, 128:] = d - hi
        return carry

    lax.fori_loop(0, half // block, trace, 0)

    both = d_ref[...].reshape(half * 8, 256).astype(jnp.bfloat16)
    for part in range(4):
        at = slice(part * tracer_ch, (part + 1) * tracer_ch)
        r_ref[:, :, at] = jnp.dot(
            both, e_ref[:, at], preferred_element_type=jnp.float32
        ).reshape(half, 8, tracer_ch)

    def interpolate(step, carry):
        for i, h in ((2 * step, 0), (2 * step, 1), (2 * step + 1, 0), (2 * step + 1, 1)):
            for v in range(lane_tiles):
                lanes = slice(v * 128, (v + 1) * 128)
                re = r_ref[i, :, (2 * h) * tracer_ch + v * 128 : (2 * h) * tracer_ch + (v + 1) * 128]
                rn = r_ref[i, :, (2 * h + 1) * tracer_ch + v * 128 : (2 * h + 1) * tracer_ch + (v + 1) * 128]
                cubic = cubic_all(re)
                linear = [linear_kernel(re - 2.0)] + linear_near(re) + [linear_kernel(re + 2.0)]
                lat = cubic_all(rn)
                inner = {-1: rn > 0.0, 1: rn < 0.0}
                acc = None
                for b in range(-2, 3):
                    line = None
                    for a in range(5):
                        if b == 0:
                            weight = cubic[a]
                        elif abs(b) == 2:
                            weight = linear[a]
                        else:
                            weight = jnp.where(inner[b], cubic[a], linear[a])
                        term = weight * s_ref[b + 2, i + half * h + a, :, lanes]
                        line = term if line is None else line + term
                    line = lat[b + 2] * line
                    acc = line if acc is None else acc + line
                out_ref[i + half * h, :, lanes] = acc.astype(out_ref.dtype)
        return carry

    lax.fori_loop(0, half // 2, interpolate, 0)


def advect(tracers_shape, wind_fields, departures, wt, ww):
    columns, total_rows, tracer_ch = tracers_shape
    levels = wind_fields.shape[-1] // 4
    bands = departures.shape[1]
    rows = total_rows // bands
    width = columns + 4
    half = columns // 2
    f32 = jnp.float32
    return pl.pallas_call(
        functools.partial(advect_kernel, columns, rows, levels),
        out_shape=jax.ShapeDtypeStruct(tracers_shape, jnp.bfloat16),
        grid_spec=pltpu.PrefetchScalarGridSpec(
            num_scalar_prefetch=1,
            grid=(bands // 2,),
            in_specs=[
                pl.BlockSpec((columns, 8, 4 * levels), lambda g, dep: (0, g, 0)),
                pl.BlockSpec(memory_space=pl.ANY),
                pl.BlockSpec(memory_space=pl.ANY),
            ],
            out_specs=pl.BlockSpec((columns, 8, tracer_ch), lambda g, dep: (0, g, 0)),
            scratch_shapes=[
                pltpu.VMEM((2, 2, width, 16, tracer_ch), jnp.bfloat16),
                pltpu.VMEM((2, 2, width, 16, 4 * levels), jnp.bfloat16),
                pltpu.VMEM((2, width, 8, tracer_ch), f32),
                pltpu.VMEM((2, width, 8, 4 * levels), f32),
                pltpu.VMEM((5, width, 8, tracer_ch), f32),
                pltpu.VMEM((3, half + 4, 8, 4 * levels), f32),
                pltpu.VMEM((half, 8, 4 * tracer_ch), f32),
                pltpu.VMEM((half, 8, 256), f32),
                pltpu.VMEM((256, 4 * tracer_ch), jnp.bfloat16),
                pltpu.SemaphoreType.DMA((2, 2, 2)),
            ],
        ),
        compiler_params=pltpu.CompilerParams(vmem_limit_bytes=60 * 1024 * 1024),
        name="advect",
    )(departures[0], wind_fields, wt, ww)

def gather_kernel(columns, chunks, t_ref, w_ref, wt_ref, ww_ref,
                  spill_t, spill_w, send, recv, spill_recv, edge_send, edge_recv, keep):
    count = lax.axis_size("lon")
    me = lax.axis_index("lon")
    core = lax.rem(me, 2)
    odd = lax.rem(me // 2, 2)
    piece = columns // chunks
    pairs = ((t_ref, wt_ref), (w_ref, ww_ref))

    def device(distance):
        return lax.rem(me + distance + count, count)

    def landing(offset, q):
        return pl.ds(2 + (offset - LOW) * columns + q * piece, piece)

    def own(flow, q, distance):
        return [
            pltpu.make_async_remote_copy(
                src_ref=local.at[pl.ds(q * piece, piece)],
                dst_ref=far.at[landing(-distance, q)],
                send_sem=send.at[flow, q, a],
                recv_sem=recv.at[-distance - LOW, q, a],
                device_id={"lon": device(distance)},
                device_id_type=MESH,
            )
            for a, (local, far) in enumerate(pairs)
        ]

    def relay(flow, q, offset, distance):
        return [
            pltpu.make_async_remote_copy(
                src_ref=far.at[landing(offset, q)],
                dst_ref=far.at[landing(offset - distance, q)],
                send_sem=send.at[flow, q, a],
                recv_sem=recv.at[offset - distance - LOW, q, a],
                device_id={"lon": device(distance)},
                device_id_type=MESH,
            )
            for a, (_, far) in enumerate(pairs)
        ]

    def arrived(offset, q):
        for a, (local, far) in enumerate(pairs):
            pltpu.make_async_remote_copy(
                src_ref=local.at[pl.ds(0, piece)],
                dst_ref=far.at[landing(offset, q)],
                send_sem=send.at[0, q, a],
                recv_sem=recv.at[offset - LOW, q, a],
                device_id={"lon": device(1)},
                device_id_type=MESH,
            ).wait_recv()

    spills = (spill_t, spill_w)

    def detour(q):
        return [
            pltpu.make_async_remote_copy(
                src_ref=local.at[pl.ds(q * piece, piece)],
                dst_ref=spills[a].at[pl.ds(q * piece, piece)],
                send_sem=send.at[3, q, a],
                recv_sem=spill_recv.at[q, a],
                device_id={"lon": device(4)},
                device_id_type=MESH,
            )
            for a, (local, _) in enumerate(pairs)
        ]

    def rejoin(q):
        return [
            pltpu.make_async_remote_copy(
                src_ref=spills[a].at[pl.ds(q * piece, piece)],
                dst_ref=far.at[landing(-2, q)],
                send_sem=send.at[4, q, a],
                recv_sem=recv.at[-2 - LOW, q, a],
                device_id={"lon": device(-2)},
                device_id_type=MESH,
            )
            for a, (_, far) in enumerate(pairs)
        ]

    def edges():
        out = []
        for a, (local, far) in enumerate(pairs):
            size = (HIGH - LOW + 1) * columns
            for side, (source, target, distance) in enumerate(
                ((columns - 2, 0, 1 - LOW), (0, 2 + size, -1 - HIGH))
            ):
                out.append(
                    pltpu.make_async_remote_copy(
                        src_ref=local.at[pl.ds(source, 2)],
                        dst_ref=far.at[pl.ds(target, 2)],
                        send_sem=edge_send.at[side, a],
                        recv_sem=edge_recv.at[side, a],
                        device_id={"lon": device(distance)},
                        device_id_type=MESH,
                    )
                )
        return out

    def stay():
        return [
            pltpu.make_async_copy(local, far.at[pl.ds(2 - LOW * columns, columns)], keep.at[a])
            for a, (local, far) in enumerate(pairs)
        ]

    sibling = 1 - 2 * core
    across = 2 - 4 * odd

    barrier = pltpu.get_barrier_semaphore()
    reach = 1 + HIGH
    for distance in range(1, reach + 1):
        for way in (distance, -distance):
            pl.semaphore_signal(
                barrier, inc=1, device_id={"lon": device(way)}, device_id_type=MESH
            )
    pl.semaphore_wait(barrier, 2 * reach)

    def begin(copies):
        for c in copies:
            c.start()

    def end(copies):
        for c in copies:
            c.wait_send()

    turns_back = odd * (1 - core)

    def other(q):
        return (2 - lax.rem(q, 3)) // 2

    def passes_on(q):
        return (1 - odd) * (1 - core) * (1 - other(q)) + odd * core * other(q)

    def crosses(q):
        return (1 - odd) * (1 - core * other(q))

    def first(q, carry):
        begin(own(1, q, across))
        begin(own(2, q, -4))

        @pl.when(core == 1)
        def _():
            begin(own(3, q, 3))

        @pl.when(turns_back * other(q) == 1)
        def _():
            begin(detour(q))

        begin(own(0, q, sibling))
        return carry

    lax.fori_loop(0, chunks, first, 0)
    begin(edges())
    begin(stay())

    def late(q):
        arrived(-across, q)
        begin(relay(7, q, -across, sibling))

    def step(q, carry):
        arrived(across, q)

        @pl.when(passes_on(q) == 1)
        def _():
            begin(relay(4, q, across, 2 * across))

        begin(relay(5, q, across, sibling))
        arrived(4, q)

        @pl.when(crosses(q) == 1)
        def _():
            begin(relay(8, q, 4, 2))

        @pl.when(core == 0)
        def _():
            begin(relay(6, q, 4, sibling))

        @pl.when(turns_back == 1)
        def _():
            arrived(-3, q)
            begin(relay(9, q, -3, -1))

        @pl.when(turns_back * other(q) == 1)
        def _():
            for c in detour(q):
                c.wait_recv()
            begin(rejoin(q))

        @pl.when(q > 0)
        def _():
            late(q - 1)

        return carry

    lax.fori_loop(0, chunks, step, 0)
    late(chunks - 1)

    def finish(q, carry):
        for offset in (-1, 1, 3):
            arrived(offset, q)
        end(own(0, q, sibling))
        end(own(1, q, across))
        end(own(2, q, -4))

        @pl.when(core == 1)
        def _():
            end(own(3, q, 3))

        @pl.when(passes_on(q) == 1)
        def _():
            end(relay(4, q, across, 2 * across))

        end(relay(5, q, across, sibling))

        @pl.when(crosses(q) == 1)
        def _():
            end(relay(8, q, 4, 2))

        @pl.when(core == 0)
        def _():
            end(relay(6, q, 4, sibling))

        @pl.when(turns_back == 1)
        def _():
            end(relay(9, q, -3, -1))

        @pl.when(turns_back * other(q) == 1)
        def _():
            end(detour(q))
            end(rejoin(q))

        @pl.when(turns_back == 0)
        def _():
            arrived(-3, q)

        end(relay(7, q, -across, sibling))
        return carry

    lax.fori_loop(0, chunks, finish, 0)
    for c in edges():
        c.wait()
    for c in stay():
        c.wait()


def gather_window(tracers, wind_fields):
    columns = tracers.shape[0]
    long = (HIGH - LOW + 1) * columns + 4
    shapes = [jax.ShapeDtypeStruct((long,) + x.shape[1:], x.dtype) for x in (tracers, wind_fields)]
    dma = pltpu.SemaphoreType.DMA
    return pl.pallas_call(
        functools.partial(gather_kernel, columns, CHUNKS),
        out_shape=shapes,
        in_specs=[pl.BlockSpec(memory_space=pl.ANY)] * 2,
        out_specs=[pl.BlockSpec(memory_space=pl.ANY)] * 2,
        scratch_shapes=[
            pltpu.VMEM(tracers.shape, tracers.dtype),
            pltpu.VMEM(wind_fields.shape, wind_fields.dtype),
            dma((10, CHUNKS, 2)),
            dma((HIGH - LOW + 1, CHUNKS, 2)),
            dma((CHUNKS, 2)),
            dma((2, 2)),
            dma((2, 2)),
            dma((2,)),
        ],
        compiler_params=pltpu.CompilerParams(collective_id=0, has_side_effects=True),
        name="gather_window",
    )(tracers, wind_fields)


def on_device(tracers, wind_fields, departures):
    wt, ww = gather_window(tracers, wind_fields)
    return advect(tracers.shape, wind_fields, departures, wt, ww)


def solution(mesh):
    placed = P(("groups", "lon"), None, None)
    return jax.shard_map(
        on_device,
        mesh=mesh,
        in_specs=(placed, placed, placed),
        out_specs=placed,
        check_vma=False,
    )
```

```python
import functools

import jax
import jax.numpy as jnp
from jax import lax
from jax.experimental import pallas as pl
from jax.experimental.pallas import tpu as pltpu
from jax.sharding import PartitionSpec as P

CAP = 4
TRAJ = 3
CLIP_BOUND = 0.95
LOW, HIGH = -3, 4
CHUNKS = 16
AHEAD = 4
LAG = 2
MESH = pl.DeviceIdType.MESH


def linear_kernel(distance):
    return jnp.maximum(1.0 - jnp.abs(distance), 0.0)


def linear_near(r):
    return [jnp.maximum(r, 0.0), 1.0 - jnp.abs(r), jnp.maximum(-r, 0.0)]


def cubic_all(r):
    t = jnp.abs(r)
    u = 1.0 - t
    v = 1.0 + t
    w = 2.0 - t
    uw = u * w
    tv = t * v
    near0 = 0.5 * (uw * v)
    near1 = 0.5 * (tv * w)
    far1 = (-1.0 / 6.0) * (uw * t)
    far2 = (-1.0 / 6.0) * (tv * u)
    pos = r > 0.0
    zero = jnp.zeros_like(t)
    return [
        jnp.where(pos, far2, zero),
        jnp.where(pos, near1, far1),
        near0,
        jnp.where(pos, far1, near1),
        jnp.where(pos, zero, far2),
    ]


def place(dep_ref, band, rows, total_rows):
    source = band - dep_ref[band, 1]
    first = source * rows - 2
    base = jnp.clip((first + 8) // 8 * 8 - 8, 0, total_rows - 16)
    return base, first - base


def advect_kernel(columns, rows, levels, dep_ref, here_ref, wt_ref, ww_ref, out_ref,
                  tbuf, wbuf, t8, w8, s_ref, p_ref, r_ref, d_ref, e_ref, sems):
    g = pl.program_id(0)
    steps = pl.num_programs(0)
    total_rows = wt_ref.shape[1]
    width = columns + 4
    tracer_ch = wt_ref.shape[2]
    lane_tiles = tracer_ch // 128
    half = columns // 2
    slot = lax.rem(g, 2)

    def copies(step, where, j):
        band = step * 2 + j
        base, _ = place(dep_ref, band, rows, total_rows)
        start = (HIGH - 1 - dep_ref[band, 0]) * columns
        at = (pl.ds(start, width), pl.ds(pl.multiple_of(base, 8), 16), slice(None))
        return (
            pltpu.make_async_copy(wt_ref.at[at], tbuf.at[where, j], sems.at[where, j, 0]),
            pltpu.make_async_copy(ww_ref.at[at], wbuf.at[where, j], sems.at[where, j, 1]),
        )

    @pl.when(g == 0)
    def _():
        for j in range(2):
            for c in copies(0, 0, j):
                c.start()
        row = lax.broadcasted_iota(jnp.int32, e_ref.shape, 0)
        col = lax.broadcasted_iota(jnp.int32, e_ref.shape, 1)
        part = col // tracer_ch
        level = (col % tracer_ch) // (tracer_ch // levels)
        hit = (row % 128) == part * levels + level
        e_ref[...] = jnp.where(hit, 1.0, 0.0).astype(e_ref.dtype)

    @pl.when(g + 1 < steps)
    def _():
        for j in range(2):
            for c in copies(g + 1, 1 - slot, j):
                c.start()

    for j in range(2):
        for c in copies(g, slot, j):
            c.wait()

    def cut(x, off):
        if off < 0:
            return jnp.concatenate([x[:, :1]] * (-off) + [x[:, : 8 + off]], axis=1)
        if off + 8 > 16:
            return jnp.concatenate([x[:, off:]] + [x[:, 15:]] * (off - 8), axis=1)
        return x[:, off : off + 8]

    for j in range(2):
        _, offset = place(dep_ref, g * 2 + j, rows, total_rows)
        for off in (-2, 2, 6, 10):

            @pl.when(offset == off)
            def _(j=j, off=off):
                def move(i, carry):
                    cs = pl.ds(i * 4, 4)
                    t8[j, cs] = cut(tbuf[slot, j, cs].astype(jnp.float32), off)
                    w8[j, cs] = cut(wbuf[slot, j, cs].astype(jnp.float32), off)
                    return carry

                lax.fori_loop(0, width // 4, move, 0)

    def interleave(a, b, ks):
        sub = lax.broadcasted_iota(jnp.int32, a.shape, a.ndim - 2)
        b = pltpu.roll(b, 4, a.ndim - 2)
        for k in ks:
            e = jnp.where((sub + 8 - k) % 8 < 4, a, b)
            yield k, (pltpu.roll(e, 8 - k, a.ndim - 2) if k else e)

    def build(i, carry):
        for u in range(4):
            col = i * 4 + u
            for k, value in interleave(t8[0, col], t8[1, col], range(5)):
                s_ref[k, col] = value
        return carry

    lax.fori_loop(0, width // 4, build, 0)

    def packed_ext(j, col):
        low = w8[j, col]
        high = w8[j, col + half]
        lane = lax.broadcasted_iota(jnp.int32, low.shape, 1)
        return jnp.where(
            lane < 64, 2.0 * low - pltpu.roll(low, 64, 1), 2.0 * pltpu.roll(high, 64, 1) - high
        )

    def build_winds(i, carry):
        for u in range(2):
            col = 1 + i * 2 + u
            for k, value in interleave(packed_ext(0, col), packed_ext(1, col), range(1, 4)):
                p_ref[k - 1, col] = value
        return carry

    lax.fori_loop(0, (half + 2) // 2, build_winds, 0)

    block = 8

    def trace(i, carry):
        first = i * block
        low = here_ref[pl.ds(first, block)].astype(jnp.float32)
        high = here_ref[pl.ds(first + half, block)].astype(jnp.float32)
        lane = lax.broadcasted_iota(jnp.int32, low.shape, 2)
        east = (lane % 64) < 32
        here = jnp.where(lane < 64, low, pltpu.roll(high, 64, 2))
        d = jnp.clip(here, -CLIP_BOUND, CLIP_BOUND)
        for _ in range(TRAJ):
            swapped = jnp.where(east, pltpu.roll(d, 96, 2), pltpu.roll(d, 32, 2))
            lon = linear_near(jnp.where(east, d, swapped))
            lat = linear_near(jnp.where(east, swapped, d))
            acc = None
            for b in range(3):
                line = None
                for a in range(3):
                    term = lon[a] * p_ref[b, pl.ds(first + 1 + a, block)]
                    line = term if line is None else line + term
                line = lat[b] * line
                acc = line if acc is None else acc + line
            d = jnp.clip(0.5 * (here + acc), -CLIP_BOUND, CLIP_BOUND)
        hi = d.astype(jnp.bfloat16).astype(jnp.float32)
        d_ref[pl.ds(first, block), :, :128] = hi
        d_ref[pl.ds(first, block), :, 128:] = d - hi
        return carry

    lax.fori_loop(0, half // block, trace, 0)

    both = d_ref[...].reshape(half * 8, 256).astype(jnp.bfloat16)
    for part in range(4):
        at = slice(part * tracer_ch, (part + 1) * tracer_ch)
        r_ref[:, :, at] = jnp.dot(
            both, e_ref[:, at], preferred_element_type=jnp.float32
        ).reshape(half, 8, tracer_ch)

    def interpolate(step, carry):
        for i, h in ((2 * step, 0), (2 * step, 1), (2 * step + 1, 0), (2 * step + 1, 1)):
            for v in range(lane_tiles):
                lanes = slice(v * 128, (v + 1) * 128)
                re = r_ref[i, :, (2 * h) * tracer_ch + v * 128 : (2 * h) * tracer_ch + (v + 1) * 128]
                rn = r_ref[i, :, (2 * h + 1) * tracer_ch + v * 128 : (2 * h + 1) * tracer_ch + (v + 1) * 128]
                cubic = cubic_all(re)
                linear = [linear_kernel(re - 2.0)] + linear_near(re) + [linear_kernel(re + 2.0)]
                lat = cubic_all(rn)
                inner = {-1: rn > 0.0, 1: rn < 0.0}
                acc = None
                for b in range(-2, 3):
                    line = None
                    for a in range(5):
                        if b == 0:
                            weight = cubic[a]
                        elif abs(b) == 2:
                            weight = linear[a]
                        else:
                            weight = jnp.where(inner[b], cubic[a], linear[a])
                        term = weight * s_ref[b + 2, i + half * h + a, :, lanes]
                        line = term if line is None else line + term
                    line = lat[b + 2] * line
                    acc = line if acc is None else acc + line
                out_ref[i + half * h, :, lanes] = acc.astype(out_ref.dtype)
        return carry

    lax.fori_loop(0, half // 2, interpolate, 0)


def advect(tracers_shape, wind_fields, departures, wt, ww):
    columns, total_rows, tracer_ch = tracers_shape
    levels = wind_fields.shape[-1] // 4
    bands = departures.shape[1]
    rows = total_rows // bands
    width = columns + 4
    half = columns // 2
    f32 = jnp.float32
    return pl.pallas_call(
        functools.partial(advect_kernel, columns, rows, levels),
        out_shape=jax.ShapeDtypeStruct(tracers_shape, jnp.bfloat16),
        grid_spec=pltpu.PrefetchScalarGridSpec(
            num_scalar_prefetch=1,
            grid=(bands // 2,),
            in_specs=[
                pl.BlockSpec((columns, 8, 4 * levels), lambda g, dep: (0, g, 0)),
                pl.BlockSpec(memory_space=pl.ANY),
                pl.BlockSpec(memory_space=pl.ANY),
            ],
            out_specs=pl.BlockSpec((columns, 8, tracer_ch), lambda g, dep: (0, g, 0)),
            scratch_shapes=[
                pltpu.VMEM((2, 2, width, 16, tracer_ch), jnp.bfloat16),
                pltpu.VMEM((2, 2, width, 16, 4 * levels), jnp.bfloat16),
                pltpu.VMEM((2, width, 8, tracer_ch), f32),
                pltpu.VMEM((2, width, 8, 4 * levels), f32),
                pltpu.VMEM((5, width, 8, tracer_ch), f32),
                pltpu.VMEM((3, half + 4, 8, 4 * levels), f32),
                pltpu.VMEM((half, 8, 4 * tracer_ch), f32),
                pltpu.VMEM((half, 8, 256), f32),
                pltpu.VMEM((256, 4 * tracer_ch), jnp.bfloat16),
                pltpu.SemaphoreType.DMA((2, 2, 2)),
            ],
        ),
        compiler_params=pltpu.CompilerParams(vmem_limit_bytes=60 * 1024 * 1024),
        name="advect",
    )(departures[0], wind_fields, wt, ww)

def gather_kernel(columns, chunks, t_ref, w_ref, wt_ref, ww_ref,
                  spill_t, spill_w, send, recv, spill_recv, edge_send, edge_recv, keep):
    count = lax.axis_size("lon")
    me = lax.axis_index("lon")
    core = lax.rem(me, 2)
    odd = lax.rem(me // 2, 2)
    piece = columns // chunks
    pairs = ((t_ref, wt_ref), (w_ref, ww_ref))

    def device(distance):
        return lax.rem(me + distance + count, count)

    def landing(offset, q):
        return pl.ds(2 + (offset - LOW) * columns + q * piece, piece)

    def own(flow, q, distance):
        return [
            pltpu.make_async_remote_copy(
                src_ref=local.at[pl.ds(q * piece, piece)],
                dst_ref=far.at[landing(-distance, q)],
                send_sem=send.at[flow, q, a],
                recv_sem=recv.at[-distance - LOW, q, a],
                device_id={"lon": device(distance)},
                device_id_type=MESH,
            )
            for a, (local, far) in enumerate(pairs)
        ]

    def relay(flow, q, offset, distance):
        return [
            pltpu.make_async_remote_copy(
                src_ref=far.at[landing(offset, q)],
                dst_ref=far.at[landing(offset - distance, q)],
                send_sem=send.at[flow, q, a],
                recv_sem=recv.at[offset - distance - LOW, q, a],
                device_id={"lon": device(distance)},
                device_id_type=MESH,
            )
            for a, (_, far) in enumerate(pairs)
        ]

    def arrived(offset, q):
        for a, (local, far) in enumerate(pairs):
            pltpu.make_async_remote_copy(
                src_ref=local.at[pl.ds(0, piece)],
                dst_ref=far.at[landing(offset, q)],
                send_sem=send.at[0, q, a],
                recv_sem=recv.at[offset - LOW, q, a],
                device_id={"lon": device(1)},
                device_id_type=MESH,
            ).wait_recv()

    spills = (spill_t, spill_w)

    def detour(q):
        return [
            pltpu.make_async_remote_copy(
                src_ref=local.at[pl.ds(q * piece, piece)],
                dst_ref=spills[a].at[pl.ds(q * piece, piece)],
                send_sem=send.at[3, q, a],
                recv_sem=spill_recv.at[q, a],
                device_id={"lon": device(4)},
                device_id_type=MESH,
            )
            for a, (local, _) in enumerate(pairs)
        ]

    def rejoin(q):
        return [
            pltpu.make_async_remote_copy(
                src_ref=spills[a].at[pl.ds(q * piece, piece)],
                dst_ref=far.at[landing(-2, q)],
                send_sem=send.at[4, q, a],
                recv_sem=recv.at[-2 - LOW, q, a],
                device_id={"lon": device(-2)},
                device_id_type=MESH,
            )
            for a, (_, far) in enumerate(pairs)
        ]

    def edges():
        out = []
        for a, (local, far) in enumerate(pairs):
            size = (HIGH - LOW + 1) * columns
            for side, (source, target, distance) in enumerate(
                ((columns - 2, 0, 1 - LOW), (0, 2 + size, -1 - HIGH))
            ):
                out.append(
                    pltpu.make_async_remote_copy(
                        src_ref=local.at[pl.ds(source, 2)],
                        dst_ref=far.at[pl.ds(target, 2)],
                        send_sem=edge_send.at[side, a],
                        recv_sem=edge_recv.at[side, a],
                        device_id={"lon": device(distance)},
                        device_id_type=MESH,
                    )
                )
        return out

    def stay():
        return [
            pltpu.make_async_copy(local, far.at[pl.ds(2 - LOW * columns, columns)], keep.at[a])
            for a, (local, far) in enumerate(pairs)
        ]

    sibling = 1 - 2 * core
    across = 2 - 4 * odd

    barrier = pltpu.get_barrier_semaphore()
    reach = 1 + HIGH
    for distance in range(1, reach + 1):
        for way in (distance, -distance):
            pl.semaphore_signal(
                barrier, inc=1, device_id={"lon": device(way)}, device_id_type=MESH
            )
    pl.semaphore_wait(barrier, 2 * reach)

    def begin(copies):
        for c in copies:
            c.start()

    def end(copies):
        for c in copies:
            c.wait_send()

    turns_back = odd * (1 - core)

    def other(q):
        return (2 - lax.rem(q, 3)) // 2

    def passes_on(q):
        return (1 - odd) * (1 - core) * (1 - other(q)) + odd * core * other(q)

    def crosses(q):
        return (1 - odd) * (1 - core * other(q))

    def first(q, carry):
        begin(own(1, q, across))
        begin(own(2, q, -4))

        @pl.when(core == 1)
        def _():
            begin(own(3, q, 3))

        @pl.when(turns_back * other(q) == 1)
        def _():
            begin(detour(q))

        begin(own(0, q, sibling))
        return carry

    lax.fori_loop(0, AHEAD, first, 0)
    begin(edges())
    begin(stay())

    def late(q):
        arrived(-across, q)
        begin(relay(7, q, -across, sibling))

    def step(q, carry):
        arrived(across, q)

        @pl.when(passes_on(q) == 1)
        def _():
            begin(relay(4, q, across, 2 * across))

        begin(relay(5, q, across, sibling))
        arrived(4, q)

        @pl.when(crosses(q) == 1)
        def _():
            begin(relay(8, q, 4, 2))

        @pl.when(core == 0)
        def _():
            begin(relay(6, q, 4, sibling))

        @pl.when(turns_back == 1)
        def _():
            arrived(-3, q)
            begin(relay(9, q, -3, -1))

        @pl.when(turns_back * other(q) == 1)
        def _():
            for c in detour(q):
                c.wait_recv()
            begin(rejoin(q))

        @pl.when(q >= LAG)
        def _():
            late(q - LAG)

        @pl.when(q + AHEAD < chunks)
        def _():
            first(q + AHEAD, 0)

        return carry

    lax.fori_loop(0, chunks, step, 0)
    for left in range(LAG, 0, -1):
        late(chunks - left)

    def finish(q, carry):
        for offset in (-1, 1, 3):
            arrived(offset, q)
        end(own(0, q, sibling))
        end(own(1, q, across))
        end(own(2, q, -4))

        @pl.when(core == 1)
        def _():
            end(own(3, q, 3))

        @pl.when(passes_on(q) == 1)
        def _():
            end(relay(4, q, across, 2 * across))

        end(relay(5, q, across, sibling))

        @pl.when(crosses(q) == 1)
        def _():
            end(relay(8, q, 4, 2))

        @pl.when(core == 0)
        def _():
            end(relay(6, q, 4, sibling))

        @pl.when(turns_back == 1)
        def _():
            end(relay(9, q, -3, -1))

        @pl.when(turns_back * other(q) == 1)
        def _():
            end(detour(q))
            end(rejoin(q))

        @pl.when(turns_back == 0)
        def _():
            arrived(-3, q)

        end(relay(7, q, -across, sibling))
        return carry

    lax.fori_loop(0, chunks, finish, 0)
    for c in edges():
        c.wait()
    for c in stay():
        c.wait()


def gather_window(tracers, wind_fields):
    columns = tracers.shape[0]
    long = (HIGH - LOW + 1) * columns + 4
    shapes = [jax.ShapeDtypeStruct((long,) + x.shape[1:], x.dtype) for x in (tracers, wind_fields)]
    dma = pltpu.SemaphoreType.DMA
    return pl.pallas_call(
        functools.partial(gather_kernel, columns, CHUNKS),
        out_shape=shapes,
        in_specs=[pl.BlockSpec(memory_space=pl.ANY)] * 2,
        out_specs=[pl.BlockSpec(memory_space=pl.ANY)] * 2,
        scratch_shapes=[
            pltpu.VMEM(tracers.shape, tracers.dtype),
            pltpu.VMEM(wind_fields.shape, wind_fields.dtype),
            dma((10, CHUNKS, 2)),
            dma((HIGH - LOW + 1, CHUNKS, 2)),
            dma((CHUNKS, 2)),
            dma((2, 2)),
            dma((2, 2)),
            dma((2,)),
        ],
        compiler_params=pltpu.CompilerParams(collective_id=0, has_side_effects=True),
        name="gather_window",
    )(tracers, wind_fields)


def on_device(tracers, wind_fields, departures):
    wt, ww = gather_window(tracers, wind_fields)
    return advect(tracers.shape, wind_fields, departures, wt, ww)


def solution(mesh):
    placed = P(("groups", "lon"), None, None)
    return jax.shard_map(
        on_device,
        mesh=mesh,
        in_specs=(placed, placed, placed),
        out_specs=placed,
        check_vma=False,
    )
```

```python
import functools

import jax
import jax.numpy as jnp
from jax import lax
from jax.experimental import pallas as pl
from jax.experimental.pallas import tpu as pltpu
from jax.sharding import PartitionSpec as P

CAP = 4
TRAJ = 3
CLIP_BOUND = 0.95
LOW, HIGH = -3, 4
CHUNKS = 16
AHEAD = 16
LAG = 8
MESH = pl.DeviceIdType.MESH


def linear_kernel(distance):
    return jnp.maximum(1.0 - jnp.abs(distance), 0.0)


def linear_near(r):
    return [jnp.maximum(r, 0.0), 1.0 - jnp.abs(r), jnp.maximum(-r, 0.0)]


def cubic_all(r):
    t = jnp.abs(r)
    u = 1.0 - t
    v = 1.0 + t
    w = 2.0 - t
    uw = u * w
    tv = t * v
    near0 = 0.5 * (uw * v)
    near1 = 0.5 * (tv * w)
    far1 = (-1.0 / 6.0) * (uw * t)
    far2 = (-1.0 / 6.0) * (tv * u)
    pos = r > 0.0
    zero = jnp.zeros_like(t)
    return [
        jnp.where(pos, far2, zero),
        jnp.where(pos, near1, far1),
        near0,
        jnp.where(pos, far1, near1),
        jnp.where(pos, zero, far2),
    ]


def place(dep_ref, band, rows, total_rows):
    source = band - dep_ref[band, 1]
    first = source * rows - 2
    base = jnp.clip((first + 8) // 8 * 8 - 8, 0, total_rows - 16)
    return base, first - base


def advect_kernel(columns, rows, levels, dep_ref, here_ref, wt_ref, ww_ref, out_ref,
                  tbuf, wbuf, t8, w8, s_ref, p_ref, r_ref, d_ref, e_ref, sems):
    g = pl.program_id(0)
    steps = pl.num_programs(0)
    total_rows = wt_ref.shape[1]
    width = columns + 4
    tracer_ch = wt_ref.shape[2]
    lane_tiles = tracer_ch // 128
    half = columns // 2
    slot = lax.rem(g, 2)

    def copies(step, where, j):
        band = step * 2 + j
        base, _ = place(dep_ref, band, rows, total_rows)
        start = (HIGH - 1 - dep_ref[band, 0]) * columns
        at = (pl.ds(start, width), pl.ds(pl.multiple_of(base, 8), 16), slice(None))
        return (
            pltpu.make_async_copy(wt_ref.at[at], tbuf.at[where, j], sems.at[where, j, 0]),
            pltpu.make_async_copy(ww_ref.at[at], wbuf.at[where, j], sems.at[where, j, 1]),
        )

    @pl.when(g == 0)
    def _():
        for j in range(2):
            for c in copies(0, 0, j):
                c.start()
        row = lax.broadcasted_iota(jnp.int32, e_ref.shape, 0)
        col = lax.broadcasted_iota(jnp.int32, e_ref.shape, 1)
        part = col // tracer_ch
        level = (col % tracer_ch) // (tracer_ch // levels)
        hit = (row % 128) == part * levels + level
        e_ref[...] = jnp.where(hit, 1.0, 0.0).astype(e_ref.dtype)

    @pl.when(g + 1 < steps)
    def _():
        for j in range(2):
            for c in copies(g + 1, 1 - slot, j):
                c.start()

    for j in range(2):
        for c in copies(g, slot, j):
            c.wait()

    def cut(x, off):
        if off < 0:
            return jnp.concatenate([x[:, :1]] * (-off) + [x[:, : 8 + off]], axis=1)
        if off + 8 > 16:
            return jnp.concatenate([x[:, off:]] + [x[:, 15:]] * (off - 8), axis=1)
        return x[:, off : off + 8]

    for j in range(2):
        _, offset = place(dep_ref, g * 2 + j, rows, total_rows)
        for off in (-2, 2, 6, 10):

            @pl.when(offset == off)
            def _(j=j, off=off):
                def move(i, carry):
                    cs = pl.ds(i * 4, 4)
                    t8[j, cs] = cut(tbuf[slot, j, cs].astype(jnp.float32), off)
                    w8[j, cs] = cut(wbuf[slot, j, cs].astype(jnp.float32), off)
                    return carry

                lax.fori_loop(0, width // 4, move, 0)

    def interleave(a, b, ks):
        sub = lax.broadcasted_iota(jnp.int32, a.shape, a.ndim - 2)
        b = pltpu.roll(b, 4, a.ndim - 2)
        for k in ks:
            e = jnp.where((sub + 8 - k) % 8 < 4, a, b)
            yield k, (pltpu.roll(e, 8 - k, a.ndim - 2) if k else e)

    def build(i, carry):
        for u in range(4):
            col = i * 4 + u
            for k, value in interleave(t8[0, col], t8[1, col], range(5)):
                s_ref[k, col] = value
        return carry

    lax.fori_loop(0, width // 4, build, 0)

    def packed_ext(j, col):
        low = w8[j, col]
        high = w8[j, col + half]
        lane = lax.broadcasted_iota(jnp.int32, low.shape, 1)
        return jnp.where(
            lane < 64, 2.0 * low - pltpu.roll(low, 64, 1), 2.0 * pltpu.roll(high, 64, 1) - high
        )

    def build_winds(i, carry):
        for u in range(2):
            col = 1 + i * 2 + u
            for k, value in interleave(packed_ext(0, col), packed_ext(1, col), range(1, 4)):
                p_ref[k - 1, col] = value
        return carry

    lax.fori_loop(0, (half + 2) // 2, build_winds, 0)

    block = 8

    def trace(i, carry):
        first = i * block
        low = here_ref[pl.ds(first, block)].astype(jnp.float32)
        high = here_ref[pl.ds(first + half, block)].astype(jnp.float32)
        lane = lax.broadcasted_iota(jnp.int32, low.shape, 2)
        east = (lane % 64) < 32
        here = jnp.where(lane < 64, low, pltpu.roll(high, 64, 2))
        d = jnp.clip(here, -CLIP_BOUND, CLIP_BOUND)
        for _ in range(TRAJ):
            swapped = jnp.where(east, pltpu.roll(d, 96, 2), pltpu.roll(d, 32, 2))
            lon = linear_near(jnp.where(east, d, swapped))
            lat = linear_near(jnp.where(east, swapped, d))
            acc = None
            for b in range(3):
                line = None
                for a in range(3):
                    term = lon[a] * p_ref[b, pl.ds(first + 1 + a, block)]
                    line = term if line is None else line + term
                line = lat[b] * line
                acc = line if acc is None else acc + line
            d = jnp.clip(0.5 * (here + acc), -CLIP_BOUND, CLIP_BOUND)
        hi = d.astype(jnp.bfloat16).astype(jnp.float32)
        d_ref[pl.ds(first, block), :, :128] = hi
        d_ref[pl.ds(first, block), :, 128:] = d - hi
        return carry

    lax.fori_loop(0, half // block, trace, 0)

    both = d_ref[...].reshape(half * 8, 256).astype(jnp.bfloat16)
    for part in range(4):
        at = slice(part * tracer_ch, (part + 1) * tracer_ch)
        r_ref[:, :, at] = jnp.dot(
            both, e_ref[:, at], preferred_element_type=jnp.float32
        ).reshape(half, 8, tracer_ch)

    def interpolate(step, carry):
        for i, h in ((2 * step, 0), (2 * step, 1), (2 * step + 1, 0), (2 * step + 1, 1)):
            for v in range(lane_tiles):
                lanes = slice(v * 128, (v + 1) * 128)
                re = r_ref[i, :, (2 * h) * tracer_ch + v * 128 : (2 * h) * tracer_ch + (v + 1) * 128]
                rn = r_ref[i, :, (2 * h + 1) * tracer_ch + v * 128 : (2 * h + 1) * tracer_ch + (v + 1) * 128]
                cubic = cubic_all(re)
                linear = [linear_kernel(re - 2.0)] + linear_near(re) + [linear_kernel(re + 2.0)]
                lat = cubic_all(rn)
                inner = {-1: rn > 0.0, 1: rn < 0.0}
                acc = None
                for b in range(-2, 3):
                    line = None
                    for a in range(5):
                        if b == 0:
                            weight = cubic[a]
                        elif abs(b) == 2:
                            weight = linear[a]
                        else:
                            weight = jnp.where(inner[b], cubic[a], linear[a])
                        term = weight * s_ref[b + 2, i + half * h + a, :, lanes]
                        line = term if line is None else line + term
                    line = lat[b + 2] * line
                    acc = line if acc is None else acc + line
                out_ref[i + half * h, :, lanes] = acc.astype(out_ref.dtype)
        return carry

    lax.fori_loop(0, half // 2, interpolate, 0)


def advect(tracers_shape, wind_fields, departures, wt, ww):
    columns, total_rows, tracer_ch = tracers_shape
    levels = wind_fields.shape[-1] // 4
    bands = departures.shape[1]
    rows = total_rows // bands
    width = columns + 4
    half = columns // 2
    f32 = jnp.float32
    return pl.pallas_call(
        functools.partial(advect_kernel, columns, rows, levels),
        out_shape=jax.ShapeDtypeStruct(tracers_shape, jnp.bfloat16),
        grid_spec=pltpu.PrefetchScalarGridSpec(
            num_scalar_prefetch=1,
            grid=(bands // 2,),
            in_specs=[
                pl.BlockSpec((columns, 8, 4 * levels), lambda g, dep: (0, g, 0)),
                pl.BlockSpec(memory_space=pl.ANY),
                pl.BlockSpec(memory_space=pl.ANY),
            ],
            out_specs=pl.BlockSpec((columns, 8, tracer_ch), lambda g, dep: (0, g, 0)),
            scratch_shapes=[
                pltpu.VMEM((2, 2, width, 16, tracer_ch), jnp.bfloat16),
                pltpu.VMEM((2, 2, width, 16, 4 * levels), jnp.bfloat16),
                pltpu.VMEM((2, width, 8, tracer_ch), f32),
                pltpu.VMEM((2, width, 8, 4 * levels), f32),
                pltpu.VMEM((5, width, 8, tracer_ch), f32),
                pltpu.VMEM((3, half + 4, 8, 4 * levels), f32),
                pltpu.VMEM((half, 8, 4 * tracer_ch), f32),
                pltpu.VMEM((half, 8, 256), f32),
                pltpu.VMEM((256, 4 * tracer_ch), jnp.bfloat16),
                pltpu.SemaphoreType.DMA((2, 2, 2)),
            ],
        ),
        compiler_params=pltpu.CompilerParams(vmem_limit_bytes=60 * 1024 * 1024),
        name="advect",
    )(departures[0], wind_fields, wt, ww)

def gather_kernel(columns, chunks, t_ref, w_ref, wt_ref, ww_ref,
                  spill_t, spill_w, send, recv, spill_recv, edge_send, edge_recv, keep):
    count = lax.axis_size("lon")
    me = lax.axis_index("lon")
    core = lax.rem(me, 2)
    odd = lax.rem(me // 2, 2)
    piece = columns // chunks
    pairs = ((t_ref, wt_ref), (w_ref, ww_ref))

    def device(distance):
        return lax.rem(me + distance + count, count)

    def landing(offset, q):
        return pl.ds(2 + (offset - LOW) * columns + q * piece, piece)

    def own(flow, q, distance):
        return [
            pltpu.make_async_remote_copy(
                src_ref=local.at[pl.ds(q * piece, piece)],
                dst_ref=far.at[landing(-distance, q)],
                send_sem=send.at[flow, q, a],
                recv_sem=recv.at[-distance - LOW, q, a],
                device_id={"lon": device(distance)},
                device_id_type=MESH,
            )
            for a, (local, far) in enumerate(pairs)
        ]

    def relay(flow, q, offset, distance):
        return [
            pltpu.make_async_remote_copy(
                src_ref=far.at[landing(offset, q)],
                dst_ref=far.at[landing(offset - distance, q)],
                send_sem=send.at[flow, q, a],
                recv_sem=recv.at[offset - distance - LOW, q, a],
                device_id={"lon": device(distance)},
                device_id_type=MESH,
            )
            for a, (_, far) in enumerate(pairs)
        ]

    def arrived(offset, q):
        for a, (local, far) in enumerate(pairs):
            pltpu.make_async_remote_copy(
                src_ref=local.at[pl.ds(0, piece)],
                dst_ref=far.at[landing(offset, q)],
                send_sem=send.at[0, q, a],
                recv_sem=recv.at[offset - LOW, q, a],
                device_id={"lon": device(1)},
                device_id_type=MESH,
            ).wait_recv()

    spills = (spill_t, spill_w)

    def detour(q):
        return [
            pltpu.make_async_remote_copy(
                src_ref=local.at[pl.ds(q * piece, piece)],
                dst_ref=spills[a].at[pl.ds(q * piece, piece)],
                send_sem=send.at[3, q, a],
                recv_sem=spill_recv.at[q, a],
                device_id={"lon": device(4)},
                device_id_type=MESH,
            )
            for a, (local, _) in enumerate(pairs)
        ]

    def rejoin(q):
        return [
            pltpu.make_async_remote_copy(
                src_ref=spills[a].at[pl.ds(q * piece, piece)],
                dst_ref=far.at[landing(-2, q)],
                send_sem=send.at[4, q, a],
                recv_sem=recv.at[-2 - LOW, q, a],
                device_id={"lon": device(-2)},
                device_id_type=MESH,
            )
            for a, (_, far) in enumerate(pairs)
        ]

    def edges():
        out = []
        for a, (local, far) in enumerate(pairs):
            size = (HIGH - LOW + 1) * columns
            for side, (source, target, distance) in enumerate(
                ((columns - 2, 0, 1 - LOW), (0, 2 + size, -1 - HIGH))
            ):
                out.append(
                    pltpu.make_async_remote_copy(
                        src_ref=local.at[pl.ds(source, 2)],
                        dst_ref=far.at[pl.ds(target, 2)],
                        send_sem=edge_send.at[side, a],
                        recv_sem=edge_recv.at[side, a],
                        device_id={"lon": device(distance)},
                        device_id_type=MESH,
                    )
                )
        return out

    def stay():
        return [
            pltpu.make_async_copy(local, far.at[pl.ds(2 - LOW * columns, columns)], keep.at[a])
            for a, (local, far) in enumerate(pairs)
        ]

    sibling = 1 - 2 * core
    across = 2 - 4 * odd

    barrier = pltpu.get_barrier_semaphore()
    reach = 1 + HIGH
    for distance in range(1, reach + 1):
        for way in (distance, -distance):
            pl.semaphore_signal(
                barrier, inc=1, device_id={"lon": device(way)}, device_id_type=MESH
            )
    pl.semaphore_wait(barrier, 2 * reach)

    def begin(copies):
        for c in copies:
            c.start()

    def end(copies):
        for c in copies:
            c.wait_send()

    turns_back = odd * (1 - core)

    def other(q):
        return (2 - lax.rem(q, 3)) // 2

    def passes_on(q):
        return (1 - odd) * (1 - core) * (1 - other(q)) + odd * core * other(q)

    def crosses(q):
        return (1 - odd) * (1 - core * other(q))

    def first(q, carry):
        begin(own(1, q, across))
        begin(own(2, q, -4))

        @pl.when(core == 1)
        def _():
            begin(own(3, q, 3))

        @pl.when(turns_back * other(q) == 1)
        def _():
            begin(detour(q))

        begin(own(0, q, sibling))
        return carry

    lax.fori_loop(0, AHEAD, first, 0)
    begin(edges())
    begin(stay())

    def late(q):
        arrived(-across, q)
        begin(relay(7, q, -across, sibling))

    def step(q, carry):
        arrived(across, q)

        @pl.when(passes_on(q) == 1)
        def _():
            begin(relay(4, q, across, 2 * across))

        begin(relay(5, q, across, sibling))
        arrived(4, q)

        @pl.when(crosses(q) == 1)
        def _():
            begin(relay(8, q, 4, 2))

        @pl.when(core == 0)
        def _():
            begin(relay(6, q, 4, sibling))

        @pl.when(turns_back == 1)
        def _():
            arrived(-3, q)
            begin(relay(9, q, -3, -1))

        @pl.when(turns_back * other(q) == 1)
        def _():
            for c in detour(q):
                c.wait_recv()
            begin(rejoin(q))

        @pl.when(q >= LAG)
        def _():
            late(q - LAG)

        @pl.when(q + AHEAD < chunks)
        def _():
            first(q + AHEAD, 0)

        return carry

    lax.fori_loop(0, chunks, step, 0)
    for left in range(LAG, 0, -1):
        late(chunks - left)

    def finish(q, carry):
        for offset in (-1, 1, 3):
            arrived(offset, q)
        end(own(0, q, sibling))
        end(own(1, q, across))
        end(own(2, q, -4))

        @pl.when(core == 1)
        def _():
            end(own(3, q, 3))

        @pl.when(passes_on(q) == 1)
        def _():
            end(relay(4, q, across, 2 * across))

        end(relay(5, q, across, sibling))

        @pl.when(crosses(q) == 1)
        def _():
            end(relay(8, q, 4, 2))

        @pl.when(core == 0)
        def _():
            end(relay(6, q, 4, sibling))

        @pl.when(turns_back == 1)
        def _():
            end(relay(9, q, -3, -1))

        @pl.when(turns_back * other(q) == 1)
        def _():
            end(detour(q))
            end(rejoin(q))

        @pl.when(turns_back == 0)
        def _():
            arrived(-3, q)

        end(relay(7, q, -across, sibling))
        return carry

    lax.fori_loop(0, chunks, finish, 0)
    for c in edges():
        c.wait()
    for c in stay():
        c.wait()


def gather_window(tracers, wind_fields):
    columns = tracers.shape[0]
    long = (HIGH - LOW + 1) * columns + 4
    shapes = [jax.ShapeDtypeStruct((long,) + x.shape[1:], x.dtype) for x in (tracers, wind_fields)]
    dma = pltpu.SemaphoreType.DMA
    return pl.pallas_call(
        functools.partial(gather_kernel, columns, CHUNKS),
        out_shape=shapes,
        in_specs=[pl.BlockSpec(memory_space=pl.ANY)] * 2,
        out_specs=[pl.BlockSpec(memory_space=pl.ANY)] * 2,
        scratch_shapes=[
            pltpu.VMEM(tracers.shape, tracers.dtype),
            pltpu.VMEM(wind_fields.shape, wind_fields.dtype),
            dma((10, CHUNKS, 2)),
            dma((HIGH - LOW + 1, CHUNKS, 2)),
            dma((CHUNKS, 2)),
            dma((2, 2)),
            dma((2, 2)),
            dma((2,)),
        ],
        compiler_params=pltpu.CompilerParams(collective_id=0, has_side_effects=True),
        name="gather_window",
    )(tracers, wind_fields)


def on_device(tracers, wind_fields, departures):
    wt, ww = gather_window(tracers, wind_fields)
    return advect(tracers.shape, wind_fields, departures, wt, ww)


def solution(mesh):
    placed = P(("groups", "lon"), None, None)
    return jax.shard_map(
        on_device,
        mesh=mesh,
        in_specs=(placed, placed, placed),
        out_specs=placed,
        check_vma=False,
    )
```
